256 devices in a mesh: depth: 64 (over y, z, core), xr: 4 (over x).
Axes of the slice: x: 4, y: 4, z: 8, core: 2. Of those that a mesh axis runs over, the one named last changes fastest.
Arguments:
- sound_field: float32 [2, 4096, 3584], P(None, 'depth', 'xr'), may hold values from -6 to 6
- index_start: float32 [4096, 3584], P('depth', 'xr'), may hold values from 0.8 to 0.98
- index_end: float32 [4096, 3584], P('depth', 'xr'), may hold values from 0.8 to 0.98
Outputs:
- stepped: float32 [2, 4096, 3584], P(None, ('depth', 'xr'))
The draws below stay inside these ranges and needn't reach their ends.
All inputs are finite; a program needn't handle non-finite values.
Results may differ from the reference program's by a relative error of at most 0.00035.
Values sent between devices are 32-bit elements; how exact they have to be, the bound alone decides.
No kernel may reach another device: no remote copies, remote signals or barrier semaphores. Data moves between devices by JAX's collectives and lax.ppermute only.
A program may use at most 128 MiB of HBM per device.

```python
import jax
import jax.numpy as jnp
from jax import lax

NZ = 4096
NY = 3584


def shard_levels(own_key, dims, pieces, low, high):
    def one(axis_at, shards_of):
        steps = jax.random.uniform(jax.random.fold_in(jax.random.fold_in(own_key, 6), axis_at), (shards_of,), jnp.float32, low / len(pieces), high / len(pieces))
        return jnp.repeat(jnp.exp(steps), dims[axis_at] // shards_of).reshape((-1,) + (1,) * (len(dims) - axis_at - 1))

    factor_of = one(*pieces[0])
    for cut in pieces[1:]:
        factor_of = factor_of * one(*cut)
    return factor_of


def noise(stream_key, extent, spread, reach, pieces=(), dtype=jnp.bfloat16):
    result = jax.random.normal(stream_key, extent, jnp.float32) * spread
    if len(pieces) > 0:
        result = shard_levels(stream_key, extent, pieces, -0.22, 0.18) * result
    return jnp.clip(result, min=-reach, max=reach).astype(dtype)


def setup_inputs(seed: int = 0) -> dict:
    streams_of = jax.random.split(jax.random.key(seed), 4)
    sound_field = noise(streams_of[0], (2, NZ, NY), 1.0, 6.0, ((1, 64), (2, 4)), jnp.float32)
    index_start = jnp.clip(0.8 + 0.18 * jax.random.uniform(streams_of[1], (NZ, NY), jnp.float32) ** shard_levels(streams_of[1], (NZ, NY), ((0, 64), (1, 4)), -0.2, 0.2), 0.8, 0.98)
    index_end = jnp.clip(0.8 + 0.18 * jax.random.uniform(streams_of[2], (NZ, NY), jnp.float32) ** shard_levels(streams_of[2], (NZ, NY), ((0, 64), (1, 4)), -0.2, 0.2), 0.8, 0.98)
    return {"sound_field": sound_field, "index_start": index_start, "index_end": index_end}


depth_stiffness = 1.6
cross_stiffness = 1.2
numer_re = 2.857
numer_im = 0.004
denom_re = 2.857
denom_im = -0.004


def complex_multiply(left_re, left_im, right_re, right_im):
    return left_re * right_re - left_im * right_im, left_re * right_im + left_im * right_re


def complex_divide(left_re, left_im, right_re, right_im):
    modulus = right_re * right_re + right_im * right_im
    return (left_re * right_re + left_im * right_im) / modulus, (left_im * right_re - left_re * right_im) / modulus


def explicit_part(values, potential, stiffness):
    border = jnp.zeros_like(values[:1])
    padded = jnp.concatenate([border, values, border], axis=0)
    return stiffness * (padded[:-2] - 2.0 * values + padded[2:]) + potential * values


def right_side(value_re, value_im, potential, stiffness):
    product_real, product_imaginary = complex_multiply(numer_re, numer_im, explicit_part(value_re, potential, stiffness), explicit_part(value_im, potential, stiffness))
    return value_re + product_real, value_im + product_imaginary


def line_solve(forcing_real, forcing_imaginary, potential, stiffness):
    offdiagonal_real = denom_re * stiffness
    offdiagonal_imaginary = denom_im * stiffness
    diagonal_real = 1.0 + denom_re * (potential - 2.0 * stiffness)
    diagonal_imaginary = denom_im * (potential - 2.0 * stiffness)

    def forward_sweep(carry_state, input_arrays):
        eliminator_real, eliminator_imaginary, filler_real, filler_imaginary = carry_state
        dgr, dgi, src_re, src_im = input_arrays
        subdiagonal_real, subdiagonal_imaginary = complex_multiply(offdiagonal_real, offdiagonal_imaginary, eliminator_real, eliminator_imaginary)
        pivot_value_real = dgr - subdiagonal_real
        pivot_value_imaginary = dgi - subdiagonal_imaginary
        updated_eliminator = complex_divide(offdiagonal_real, offdiagonal_imaginary, pivot_value_real, pivot_value_imaginary)
        carried_re, carried_im = complex_multiply(offdiagonal_real, offdiagonal_imaginary, filler_real, filler_imaginary)
        updated_filler = complex_divide(src_re - carried_re, src_im - carried_im, pivot_value_real, pivot_value_imaginary)
        sweep_result = (updated_eliminator[0], updated_eliminator[1], updated_filler[0], updated_filler[1])
        return sweep_result, sweep_result

    empty_line_row = jnp.zeros_like(forcing_real[0])
    start_row = (empty_line_row, empty_line_row, empty_line_row, empty_line_row)
    unused_item, (eliminator_real, eliminator_imaginary, filler_real, filler_imaginary) = lax.scan(forward_sweep, start_row, (diagonal_real, diagonal_imaginary, forcing_real, forcing_imaginary))

    def backward_sweep(carry_state, input_arrays):
        following_real, following_imaginary = carry_state
        cell_eliminator_real, cell_eliminator_imaginary, cell_filler_real, cell_filler_imaginary = input_arrays
        product_real, product_imaginary = complex_multiply(cell_eliminator_real, cell_eliminator_imaginary, following_real, following_imaginary)
        sweep_result = (cell_filler_real - product_real, cell_filler_imaginary - product_imaginary)
        return sweep_result, sweep_result

    unused_item, (unknown_real, unknown_imaginary) = lax.scan(backward_sweep, (empty_line_row, empty_line_row), (eliminator_real, eliminator_imaginary, filler_real, filler_imaginary), reverse=True)
    return unknown_real, unknown_imaginary


def reference(sound_field, index_start, index_end):
    depth_potential = (index_start - 1.0) * 0.5
    cross_potential = (index_end - 1.0) * 0.5
    forcing_real, forcing_imaginary = right_side(sound_field[0], sound_field[1], depth_potential, depth_stiffness)
    middle_re, middle_im = line_solve(forcing_real, forcing_imaginary, depth_potential, depth_stiffness)
    cross_re, cross_im = right_side(middle_re.T, middle_im.T, cross_potential.T, cross_stiffness)
    final_re, final_im = line_solve(cross_re, cross_im, cross_potential.T, cross_stiffness)
    return jnp.stack([final_re.T, final_im.T])
```

```python
import jax
import jax.numpy as jnp
from jax import lax
from jax.experimental import pallas as pl
from jax.experimental.pallas import tpu as pltpu
from jax.sharding import Mesh
from jax.sharding import PartitionSpec as P

DEPTH = ("y", "z", "c")

DEPTH_STIFFNESS = 1.6
CROSS_STIFFNESS = 1.2
NUMER = complex(2.857, 0.004)
DENOM = complex(2.857, -0.004)

MIX = NUMER / DENOM

SUB = 8
LANE = 128
CELLS = 64
PARTS = 12


def constants(stiffness):
    slope = -0.5 / stiffness
    base = 2.0 - (1.0 / DENOM).real / stiffness - slope
    swing = -(1.0 / DENOM).imag / stiffness
    gain = (1.0 - MIX) / (stiffness * DENOM)
    return base, slope, swing, gain


def mul(a, b):
    return a[0] * b[0] - a[1] * b[1], a[0] * b[1] + a[1] * b[0]


def add(a, b):
    return a[0] + b[0], a[1] + b[1]


def sub(a, b):
    return a[0] - b[0], a[1] - b[1]


def neg(a):
    return -a[0], -a[1]


def scaled(a, s):
    return a[0] * s, a[1] * s


def pick(flag, yes, no):
    return [(jnp.where(flag, p[0], q[0]), jnp.where(flag, p[1], q[1])) for p, q in zip(yes, no)]


def compose(early, late):
    a00, a10, a01, a11, r0, r1 = early
    b00, b10, b01, b11, s0, s1 = late
    return [
        add(mul(b00, a00), mul(b01, a10)),
        add(mul(b10, a00), mul(b11, a10)),
        add(mul(b00, a01), mul(b01, a11)),
        add(mul(b10, a01), mul(b11, a11)),
        add(r0, add(mul(a00, s0), mul(a10, s1))),
        add(r1, add(mul(a01, s0), mul(a11, s1))),
    ]


def normal(state):
    f0, f1, g = state
    size = jnp.maximum(
        jnp.maximum(jnp.abs(f0[0]), jnp.abs(f0[1])), jnp.maximum(jnp.abs(f1[0]), jnp.abs(f1[1]))
    )
    scale = 1.0 / size
    return [scaled(f0, scale), scaled(f1, scale), scaled(g, scale)]


def advance(state, span):
    f0, f1, g = state
    t00, t10, t01, t11, s0, s1 = span
    return [
        add(mul(t00, f0), mul(t01, f1)),
        add(mul(t10, f0), mul(t11, f1)),
        add(g, add(mul(f0, s0), mul(f1, s1))),
    ]


def retreat(state, span):
    p0, p1, h = state
    t00, t10, t01, t11, s0, s1 = span
    q0 = sub(mul(t11, p0), mul(t01, p1))
    q1 = sub(mul(t00, p1), mul(t10, p0))
    return [q0, q1, add(h, add(mul(q0, s0), mul(q1, s1)))]


def meet(left, right):
    f0, f1, g = left
    p0, p1, h = right
    det = sub(mul(f1, p0), mul(f0, p1))
    scale = -1.0 / (det[0] * det[0] + det[1] * det[1])
    inverse = (det[0] * scale, -det[1] * scale)
    v0 = mul(add(mul(f0, h), mul(p0, g)), inverse)
    v1 = mul(add(mul(g, p1), mul(f1, h)), inverse)
    return v0, v1


def ends(like):
    zero = jnp.zeros_like(like)
    one = zero + 1.0
    return [(zero, zero), (one, zero), (zero, zero)], [(one, zero), (zero, zero), (zero, zero)]


def read(ref):
    return [(ref[2 * i], ref[2 * i + 1]) for i in range(PARTS // 2)]


def write(ref, span):
    for i, part in enumerate(span):
        ref[2 * i] = part[0]
        ref[2 * i + 1] = part[1]


def rows(k):
    return pl.ds(SUB * k, SUB)


def march_span(source, curve, swing):
    zero = jnp.zeros((SUB, LANE), jnp.float32)
    one = zero + 1.0
    past = [(one, zero), (zero, zero)]
    now = [(zero, zero), (one, zero)]
    sums = [(zero, zero), (zero, zero)]
    for k in range(CELLS):
        u = source[0, rows(k), :], source[1, rows(k), :]
        c = curve[rows(k), :]
        for i in range(2):
            p, n = past[i], now[i]
            sums[i] = add(sums[i], mul(n, u))
            new = (c * n[0] - (swing * n[1] + p[0]), c * n[1] + (swing * n[0] - p[1]))
            past[i], now[i] = n, new
    return [past[0], now[0], past[1], now[1], sums[0], sums[1]]


def march_solution(source, curve, swing, gain, v0, v1, target):
    past, now = v0, v1
    for k in range(CELLS):
        u = source[0, rows(k), :], source[1, rows(k), :]
        c = curve[rows(k), :]
        target[0, rows(k), :] = (MIX.real * u[0] - MIX.imag * u[1]) + (gain.real * now[0] - gain.imag * now[1])
        target[1, rows(k), :] = (MIX.real * u[1] + MIX.imag * u[0]) + (gain.real * now[1] + gain.imag * now[0])
        new = (
            c * now[0] + (u[0] - past[0] - swing * now[1]),
            c * now[1] + (u[1] - past[1] + swing * now[0]),
        )
        past, now = now, new


def open_kernel(field, start, end, span, source, curve, end0, end1, end2, end3):
    base, slope, swing, _ = constants(DEPTH_STIFFNESS)
    xbase, xslope, _, _ = constants(CROSS_STIFFNESS)
    tiles = field.shape[2] // LANE
    x = lax.axis_index("xr")
    for t in range(SUB):
        spread = pl.ds(t, CELLS, stride=SUB)
        if t < tiles:
            cols = slice(t * LANE, (t + 1) * LANE)
            source[0, spread, :] = field[0, :, cols]
            source[1, spread, :] = field[1, :, cols]
            curve[spread, :] = base + slope * start[:, cols]
        else:
            zero = jnp.zeros((CELLS, LANE), jnp.float32)
            source[0, spread, :] = zero
            source[1, spread, :] = zero
            curve[spread, :] = zero + (base + 0.9 * slope)
    write(span, march_span(source, curve, swing))
    piece = CELLS // 4
    for d, target in enumerate((end0, end1, end2, end3)):
        first = pl.multiple_of((x ^ d) * piece, piece)
        for t in range(SUB):
            spread = pl.ds(t, piece, stride=SUB)
            if t < tiles:
                cols = slice(t * LANE, (t + 1) * LANE)
                target[spread, :] = xbase + xslope * end[pl.ds(first, piece), cols]
            else:
                target[spread, :] = jnp.zeros((piece, LANE), jnp.float32) + (xbase + 0.9 * xslope)


def pair_kernel(axis, bit, own, other, total):
    upper = ((lax.axis_index(axis) >> bit) & 1) == 1
    a, b = read(own), read(other)
    write(total, compose(pick(upper, b, a), pick(upper, a, b)))


def quad_kernel(axis, own, other1, other2, other3, total):
    place = lax.axis_index(axis)
    odd = (place & 1) == 1
    high = (place & 2) == 2
    a, r1, r2, r3 = read(own), read(other1), read(other2), read(other3)
    mine = compose(pick(odd, r1, a), pick(odd, a, r1))
    theirs = compose(pick(odd, r3, r2), pick(odd, r2, r3))
    write(total, compose(pick(high, theirs, mine), pick(high, mine, theirs)))


def descend_pair(left, right, upper, other):
    return (
        pick(upper, normal(advance(left, other)), left),
        pick(upper, right, normal(retreat(right, other))),
    )


def descend_quad(left, right, place, r1, r2, r3):
    odd = (place & 1) == 1
    high = (place & 2) == 2
    first, second = pick(odd, r3, r2), pick(odd, r2, r3)
    left = pick(high, normal(advance(normal(advance(left, first)), second)), left)
    right = pick(high, right, normal(retreat(normal(retreat(right, second)), first)))
    return descend_pair(left, right, odd, r1)


def close_kernel(source, curve, own, c1, z1, z2, z3, z4, y1, y2, y3, mid0, mid1, mid2, mid3, whole):
    _, _, swing, gain = constants(DEPTH_STIFFNESS)
    x, y, z, c = (lax.axis_index(name) for name in ("xr", "y", "z", "c"))
    left, right = ends(own[0])
    left, right = descend_quad(left, right, y, read(y1), read(y2), read(y3))
    left, right = descend_pair(left, right, (z & 4) == 4, read(z4))
    left, right = descend_quad(left, right, z & 3, read(z1), read(z2), read(z3))
    left, right = descend_pair(left, right, c == 1, read(c1))
    right = normal(retreat(right, read(own)))
    v0, v1 = meet(left, right)
    march_solution(source, curve, swing, gain, v0, v1, whole)
    piece = SUB * CELLS // 4
    for d, target in enumerate((mid0, mid1, mid2, mid3)):
        first = pl.multiple_of((x ^ d) * piece, piece)
        target[...] = whole[:, pl.ds(first, piece), :]


def cross_kernel(mid0, mid1, mid2, mid3, end0, end1, end2, end3, out, turned, source, curve):
    _, _, swing, gain = constants(CROSS_STIFFNESS)
    tiles = out.shape[2] // LANE // 4
    x = lax.axis_index("xr")
    for d, (mid, end) in enumerate(((mid0, end0), (mid1, end1), (mid2, end2), (mid3, end3))):
        at = x ^ d
        turned[at, 0] = mid[0].T
        turned[at, 1] = mid[1].T
        turned[at, 2] = end[...].T
    for q in range(4):
        for h in range(2):
            spread = pl.ds(2 * q + h, CELLS, stride=SUB)
            half = slice(CELLS * h, CELLS * (h + 1))
            source[0, spread, :] = turned[q, 0, half, :]
            source[1, spread, :] = turned[q, 1, half, :]
            curve[spread, :] = turned[q, 2, half, :]
    span = march_span(source, curve, swing)
    lane = lax.broadcasted_iota(jnp.int32, (SUB, LANE), 1)
    row = lax.broadcasted_iota(jnp.int32, (SUB, LANE), 0)
    zero = jnp.zeros((SUB, LANE), jnp.float32)
    one = zero + 1.0
    unit = [(one, zero), (zero, zero), (zero, zero), (one, zero), (zero, zero), (zero, zero)]
    span = pick((lane & 7) >= tiles, unit, span)
    levels = []
    total = span
    for axis, step in ((0, 1), (1, 1), (1, 2), (1, 4), (0, 2), (0, 4)):
        size = SUB if axis == 0 else LANE
        upper = ((row if axis == 0 else lane) & step) == step

        def swapped(v, axis=axis, step=step, size=size, upper=upper):
            down = pltpu.roll(v, step, axis)
            if 2 * step == size:
                return down
            return jnp.where(upper, down, pltpu.roll(v, size - step, axis))

        other = [(swapped(p[0]), swapped(p[1])) for p in total]
        levels.append((upper, other))
        if len(levels) < 6:
            total = compose(pick(upper, other, total), pick(upper, total, other))
    left, right = ends(zero)
    for upper, other in reversed(levels):
        left, right = descend_pair(left, right, upper, other)
    right = normal(retreat(right, span))
    v0, v1 = meet(left, right)
    march_solution(source, curve, swing, gain, v0, v1, source)
    for part in range(2):
        for q in range(4):
            halves = [source[part, pl.ds(2 * q + h, CELLS, stride=SUB), :] for h in range(2)]
            turned[q, part] = jnp.concatenate(halves, axis=0).T
            for t in range(tiles):
                cols = slice((q * tiles + t) * LANE, (q * tiles + t + 1) * LANE)
                out[part, :, cols] = turned[q, part, pl.ds(t, CELLS // 4, stride=SUB), :]


def shaped(*shape):
    return jax.ShapeDtypeStruct(shape, jnp.float32)


def call(kernel, name, outs, scratch=(), flops=100000):
    return pl.pallas_call(
        kernel,
        name=name,
        out_shape=outs,
        scratch_shapes=list(scratch),
        cost_estimate=pl.CostEstimate(flops=flops, bytes_accessed=1000000, transcendentals=0),
    )


def swap(value, axis, pairs):
    return lax.ppermute(value, axis, pairs)


def local(sound_field, index_start, index_end):
    span_shape = shaped(PARTS, SUB, LANE)
    cells = SUB * CELLS
    piece = cells // 4
    opened = call(
        open_kernel,
        "open",
        [span_shape, shaped(2, cells, LANE), shaped(cells, LANE)] + [shaped(piece, LANE)] * 4,
    )(sound_field, index_start, index_end)
    own, source, curve = opened[:3]
    ends_out = opened[3:]

    def flip(value, axis, d):
        return swap(value, axis, [(i, i ^ d) for i in range(lax.axis_size(axis))])

    def pair(axis, bit, a, b):
        return call(lambda *refs: pair_kernel(axis, bit, *refs), "pair", span_shape)(a, b)

    def quad(axis, a, others):
        return call(lambda *refs: quad_kernel(axis, *refs), "quad", span_shape)(a, *others)

    c1 = flip(own, "c", 1)
    total = pair("c", 0, own, c1)
    zs = [flip(total, "z", d) for d in (1, 2, 3)]
    total = quad("z", total, zs)
    z4 = swap(total, "z", [(i, 7 - i) for i in range(8)])
    total = pair("z", 2, total, z4)
    ys = [flip(total, "y", d) for d in (1, 2, 3)]
    end_in = [ends_out[0]] + [flip(ends_out[d], "xr", d) for d in (1, 2, 3)]
    mids = call(
        close_kernel,
        "close",
        [shaped(2, piece, LANE)] * 4,
        [pltpu.VMEM((2, cells, LANE), jnp.float32)],
    )(source, curve, own, c1, *zs, z4, *ys)
    mid_in = [mids[0]] + [flip(mids[d], "xr", d) for d in (1, 2, 3)]
    lines = CELLS // 4
    width = 4 * sound_field.shape[2]
    return call(
        cross_kernel,
        "cross",
        shaped(2, lines, width),
        [
            pltpu.VMEM((4, 3, LANE, LANE), jnp.float32),
            pltpu.VMEM((2, cells, LANE), jnp.float32),
            pltpu.VMEM((cells, LANE), jnp.float32),
        ],
    )(*mid_in, *end_in)


def solution(mesh):
    split = Mesh(mesh.devices.reshape(4, 8, 2, mesh.shape["xr"]), DEPTH + ("xr",))
    in_specs = (P(None, DEPTH, "xr"), P(DEPTH, "xr"), P(DEPTH, "xr"))
    out_specs = P(None, DEPTH + ("xr",), None)
    return jax.shard_map(local, mesh=split, in_specs=in_specs, out_specs=out_specs, check_vma=False)
```

```python
import jax
import jax.numpy as jnp
from jax import lax
from jax.experimental import pallas as pl
from jax.experimental.pallas import tpu as pltpu
from jax.sharding import Mesh
from jax.sharding import PartitionSpec as P

DEPTH = ("y", "z", "c")

DEPTH_STIFFNESS = 1.6
CROSS_STIFFNESS = 1.2
NUMER = complex(2.857, 0.004)
DENOM = complex(2.857, -0.004)

MIX = NUMER / DENOM

SUB = 8
LANE = 128
CELLS = 64
PARTS = 12


def constants(stiffness):
    slope = -0.5 / stiffness
    base = 2.0 - (1.0 / DENOM).real / stiffness - slope
    swing = -(1.0 / DENOM).imag / stiffness
    gain = (1.0 - MIX) / (stiffness * DENOM)
    return base, slope, swing, gain


def mul(a, b):
    return a[0] * b[0] - a[1] * b[1], a[0] * b[1] + a[1] * b[0]


def add(a, b):
    return a[0] + b[0], a[1] + b[1]


def sub(a, b):
    return a[0] - b[0], a[1] - b[1]


def scaled(a, s):
    return a[0] * s, a[1] * s


def pick(flag, yes, no):
    return [(jnp.where(flag, p[0], q[0]), jnp.where(flag, p[1], q[1])) for p, q in zip(yes, no)]


def compose(early, late):
    a00, a10, a01, a11, r0, r1 = early
    b00, b10, b01, b11, s0, s1 = late
    return [
        add(mul(b00, a00), mul(b01, a10)),
        add(mul(b10, a00), mul(b11, a10)),
        add(mul(b00, a01), mul(b01, a11)),
        add(mul(b10, a01), mul(b11, a11)),
        add(r0, add(mul(a00, s0), mul(a10, s1))),
        add(r1, add(mul(a01, s0), mul(a11, s1))),
    ]


def normal(state):
    f0, f1, g = state
    size = jnp.maximum(
        jnp.maximum(jnp.abs(f0[0]), jnp.abs(f0[1])), jnp.maximum(jnp.abs(f1[0]), jnp.abs(f1[1]))
    )
    scale = 1.0 / size
    return [scaled(f0, scale), scaled(f1, scale), scaled(g, scale)]


def advance(state, span):
    f0, f1, g = state
    t00, t10, t01, t11, s0, s1 = span
    return [
        add(mul(t00, f0), mul(t01, f1)),
        add(mul(t10, f0), mul(t11, f1)),
        add(g, add(mul(f0, s0), mul(f1, s1))),
    ]


def retreat(state, span):
    p0, p1, h = state
    t00, t10, t01, t11, s0, s1 = span
    q0 = sub(mul(t11, p0), mul(t01, p1))
    q1 = sub(mul(t00, p1), mul(t10, p0))
    return [q0, q1, add(h, add(mul(q0, s0), mul(q1, s1)))]


def meet(left, right):
    f0, f1, g = left
    p0, p1, h = right
    det = sub(mul(f1, p0), mul(f0, p1))
    scale = -1.0 / (det[0] * det[0] + det[1] * det[1])
    inverse = (det[0] * scale, -det[1] * scale)
    v0 = mul(add(mul(f0, h), mul(p0, g)), inverse)
    v1 = mul(add(mul(g, p1), mul(f1, h)), inverse)
    return v0, v1


def ends(like):
    zero = jnp.zeros_like(like)
    one = zero + 1.0
    return [(zero, zero), (one, zero), (zero, zero)], [(one, zero), (zero, zero), (zero, zero)]


def read(ref):
    return [(ref[2 * i], ref[2 * i + 1]) for i in range(PARTS // 2)]


def write(ref, span):
    for i, part in enumerate(span):
        ref[2 * i] = part[0]
        ref[2 * i + 1] = part[1]


def rows(k):
    return pl.ds(SUB * k, SUB)


def march_span(source, curve, swing, every=CELLS):
    zero = jnp.zeros((SUB, LANE), jnp.float32)
    one = zero + 1.0
    past = [(one, zero), (zero, zero)]
    now = [(zero, zero), (one, zero)]
    sums = [(zero, zero), (zero, zero)]
    spans = []
    for k in range(CELLS):
        u = source[0, rows(k), :], source[1, rows(k), :]
        c = curve[rows(k), :]
        for i in range(2):
            p, n = past[i], now[i]
            sums[i] = add(sums[i], mul(n, u))
            new = (c * n[0] - (swing * n[1] + p[0]), c * n[1] + (swing * n[0] - p[1]))
            past[i], now[i] = n, new
        if (k + 1) % every == 0:
            spans.append([past[0], now[0], past[1], now[1], sums[0], sums[1]])
    return spans


def march_solution(source, curve, swing, gain, v0, v1, target, count=CELLS):
    past, now = v0, v1
    for k in range(count):
        u, c = source(k), curve(k)
        target(
            k,
            (MIX.real * u[0] - MIX.imag * u[1]) + (gain.real * now[0] - gain.imag * now[1]),
            (MIX.real * u[1] + MIX.imag * u[0]) + (gain.real * now[1] + gain.imag * now[0]),
        )
        new = (
            c * now[0] + (u[0] - past[0] - swing * now[1]),
            c * now[1] + (u[1] - past[1] + swing * now[0]),
        )
        past, now = now, new


def carry(span, v0, v1):
    t00, t10, t01, t11, s0, s1 = span
    a, b = sub(v0, s1), add(v1, s0)
    return add(mul(t00, a), mul(t01, b)), add(mul(t10, a), mul(t11, b))


def open_kernel(field, start, end, own, snap, *rest):
    packs, (source, curve, field_in, start_in, end_in, sems) = rest[:4], rest[4:]
    base, slope, swing, _ = constants(DEPTH_STIFFNESS)
    xbase, xslope, _, _ = constants(CROSS_STIFFNESS)
    loads = [
        pltpu.make_async_copy(a, b, sems.at[i])
        for i, (a, b) in enumerate(((field, field_in), (start, start_in), (end, end_in)))
    ]
    for load in loads:
        load.start()
    tiles = field.shape[2] // LANE
    x = lax.axis_index("xr")
    zero = jnp.zeros((CELLS, LANE), jnp.float32)
    for t in range(tiles, SUB):
        spread = pl.ds(t, CELLS, stride=SUB)
        source[0, spread, :] = zero
        source[1, spread, :] = zero
        curve[0, spread, :] = zero + (base + 0.9 * slope)
        curve[1, spread, :] = zero + (xbase + 0.9 * xslope)
    loads[1].wait()
    for t in range(tiles):
        spread, cols = pl.ds(t, CELLS, stride=SUB), slice(t * LANE, (t + 1) * LANE)
        curve[0, spread, :] = base + slope * start_in[:, cols]
    loads[0].wait()
    for t in range(tiles):
        spread, cols = pl.ds(t, CELLS, stride=SUB), slice(t * LANE, (t + 1) * LANE)
        source[0, spread, :] = field_in[0, :, cols]
        source[1, spread, :] = field_in[1, :, cols]
    spans = march_span(source, curve.at[0], swing, CELLS // 4)
    write(own, spans[3])
    for i in range(3):
        write(snap.at[i], spans[i])
    loads[2].wait()
    for t in range(tiles):
        spread, cols = pl.ds(t, CELLS, stride=SUB), slice(t * LANE, (t + 1) * LANE)
        curve[1, spread, :] = xbase + xslope * end_in[:, cols]
    piece = SUB * CELLS // 4
    for d, pack in enumerate(packs):
        first = pl.multiple_of((x ^ d) * piece, piece)
        pack[0:2] = source[:, pl.ds(first, piece), :]
        pack[2:4] = curve[:, pl.ds(first, piece), :]


def turn_kernel(pack, turned):
    turned[...] = pack[3].T


def pair_kernel(axis, bit, own, other, total):
    upper = ((lax.axis_index(axis) >> bit) & 1) == 1
    a, b = read(own), read(other)
    write(total, compose(pick(upper, b, a), pick(upper, a, b)))


def quad_kernel(axis, own, other1, other2, other3, total):
    place = lax.axis_index(axis)
    odd = (place & 1) == 1
    high = (place & 2) == 2
    a, r1, r2, r3 = read(own), read(other1), read(other2), read(other3)
    mine = compose(pick(odd, r1, a), pick(odd, a, r1))
    theirs = compose(pick(odd, r3, r2), pick(odd, r2, r3))
    write(total, compose(pick(high, theirs, mine), pick(high, mine, theirs)))


def descend_pair(left, right, upper, other):
    return (
        pick(upper, normal(advance(left, other)), left),
        pick(upper, right, normal(retreat(right, other))),
    )


def descend_quad(left, right, place, r1, r2, r3):
    odd = (place & 1) == 1
    high = (place & 2) == 2
    first, second = pick(odd, r3, r2), pick(odd, r2, r3)
    left = pick(high, normal(advance(normal(advance(left, first)), second)), left)
    right = pick(high, right, normal(retreat(normal(retreat(right, second)), first)))
    return descend_pair(left, right, odd, r1)


def close_kernel(own, snap, c1, z1, z2, z3, z4, y1, y2, y3, bound0, bound1, bound2, bound3, bounds):
    x, y, z, c = (lax.axis_index(name) for name in ("xr",) + DEPTH)
    left, right = ends(own[0])
    left, right = descend_quad(left, right, y, read(y1), read(y2), read(y3))
    left, right = descend_pair(left, right, (z & 4) == 4, read(z4))
    left, right = descend_quad(left, right, z & 3, read(z1), read(z2), read(z3))
    left, right = descend_pair(left, right, c == 1, read(c1))
    right = normal(retreat(right, read(own)))
    v0, v1 = meet(left, right)
    for i in range(4):
        a, b = carry(read(snap.at[i - 1]), v0, v1) if i else (v0, v1)
        for j, part in enumerate((a[0], a[1], b[0], b[1])):
            bounds[i, j] = part
    for d, bound in enumerate((bound0, bound1, bound2, bound3)):
        bound[...] = bounds[x ^ d]


def cross_kernel(*refs):
    bounds, packs, turns, (result, mid, turned, source, curve, out, sems) = (
        refs[:4], refs[4:8], refs[8:11], refs[11:],
    )
    _, _, swing, gain = constants(DEPTH_STIFFNESS)
    tiles = result.shape[2] // LANE // 4
    x = lax.axis_index("xr")
    lines = CELLS // 4
    for d in range(4):
        pack, bound = packs[d], bounds[d]

        def put(k, re, im, d=d):
            mid[d, 0, rows(k), :] = re
            mid[d, 1, rows(k), :] = im

        march_solution(
            lambda k: (pack[0, rows(k), :], pack[1, rows(k), :]), lambda k: pack[2, rows(k), :],
            swing, gain, (bound[0], bound[1]), (bound[2], bound[3]), put, lines,
        )
    for d in range(4):
        at = x ^ d
        turned[at, 0] = mid[d, 0].T
        turned[at, 1] = mid[d, 1].T
        turned[at, 2] = turns[d][...] if d < 3 else packs[d][3].T
    _, _, swing, gain = constants(CROSS_STIFFNESS)
    for q in range(4):
        for h in range(2):
            spread = pl.ds(2 * q + h, CELLS, stride=SUB)
            half = slice(CELLS * h, CELLS * (h + 1))
            source[0, spread, :] = turned[q, 0, half, :]
            source[1, spread, :] = turned[q, 1, half, :]
            curve[spread, :] = turned[q, 2, half, :]
    (span,) = march_span(source, curve, swing)
    lane = lax.broadcasted_iota(jnp.int32, (SUB, LANE), 1)
    row = lax.broadcasted_iota(jnp.int32, (SUB, LANE), 0)
    zero = jnp.zeros((SUB, LANE), jnp.float32)
    one = zero + 1.0
    unit = [(one, zero), (zero, zero), (zero, zero), (one, zero), (zero, zero), (zero, zero)]
    span = pick((lane & 7) >= tiles, unit, span)
    levels = []
    total = span
    for axis, step in ((0, 1), (1, 1), (1, 2), (1, 4), (0, 2), (0, 4)):
        size = SUB if axis == 0 else LANE
        upper = ((row if axis == 0 else lane) & step) == step

        def swapped(v, axis=axis, step=step, size=size, upper=upper):
            down = pltpu.roll(v, step, axis)
            if 2 * step == size:
                return down
            return jnp.where(upper, down, pltpu.roll(v, size - step, axis))

        other = [(swapped(p[0]), swapped(p[1])) for p in total]
        levels.append((upper, other))
        if len(levels) < 6:
            total = compose(pick(upper, other, total), pick(upper, total, other))
    left, right = ends(zero)
    for upper, other in reversed(levels):
        left, right = descend_pair(left, right, upper, other)
    right = normal(retreat(right, span))
    v0, v1 = meet(left, right)

    def put(k, re, im):
        source[0, rows(k), :] = re
        source[1, rows(k), :] = im

    march_solution(
        lambda k: (source[0, rows(k), :], source[1, rows(k), :]), lambda k: curve[rows(k), :],
        swing, gain, v0, v1, put,
    )
    stores = []
    for part in range(2):
        for q in range(4):
            halves = [source[part, pl.ds(2 * q + h, CELLS, stride=SUB), :] for h in range(2)]
            turned[q, part] = jnp.concatenate(halves, axis=0).T
            for t in range(tiles):
                cols = slice((q * tiles + t) * LANE, (q * tiles + t + 1) * LANE)
                out[part, :, cols] = turned[q, part, pl.ds(t, lines, stride=SUB), :]
            whole = pl.ds(q * tiles * LANE, tiles * LANE)
            store = pltpu.make_async_copy(
                out.at[part, :, whole], result.at[part, :, whole], sems.at[4 * part + q]
            )
            store.start()
            stores.append(store)
    for store in stores:
        store.wait()


def shaped(*shape):
    return jax.ShapeDtypeStruct(shape, jnp.float32)


def call(kernel, outs, scratch=(), far_in=False, far_out=False):
    far, here = pl.BlockSpec(memory_space=pltpu.HBM), pl.BlockSpec(memory_space=pltpu.VMEM)
    out_specs = [far if far_out else here] * len(outs) if isinstance(outs, list) else (far if far_out else here)

    def run(*values):
        return pl.pallas_call(
            kernel,
            out_shape=outs,
            in_specs=[far if far_in else here] * len(values),
            out_specs=out_specs,
            scratch_shapes=list(scratch),
            compiler_params=pltpu.CompilerParams(vmem_limit_bytes=8 << 20),
            cost_estimate=pl.CostEstimate(flops=100000, bytes_accessed=1000000, transcendentals=0),
        )(*values)

    return run


def local(sound_field, index_start, index_end):
    span_shape = shaped(PARTS, SUB, LANE)
    cells = SUB * CELLS
    piece = cells // 4
    inputs = (sound_field, index_start, index_end)
    own, snap, *packs = call(
        open_kernel,
        [span_shape, shaped(3, PARTS, SUB, LANE)] + [shaped(4, piece, LANE)] * 4,
        [pltpu.VMEM((2, cells, LANE), jnp.float32)] * 2
        + [pltpu.VMEM(v.shape, jnp.float32) for v in inputs]
        + [pltpu.SemaphoreType.DMA((3,))],
        far_in=True,
    )(*(pltpu.with_memory_space_constraint(v, pltpu.HBM) for v in inputs))

    def flip(value, axis, d):
        return lax.ppermute(value, axis, [(i, i ^ d) for i in range(lax.axis_size(axis))])

    def pair(axis, bit, a, b):
        return call(lambda *refs: pair_kernel(axis, bit, *refs), span_shape)(a, b)

    def quad(axis, a, others):
        return call(lambda *refs: quad_kernel(axis, *refs), span_shape)(a, *others)

    c1 = flip(own, "c", 1)
    total = pair("c", 0, own, c1)
    zs = [flip(total, "z", d) for d in (1, 2, 3)]
    total = quad("z", total, zs)
    z4 = lax.ppermute(total, "z", [(i, 7 - i) for i in range(8)])
    total = pair("z", 2, total, z4)
    ys = [flip(total, "y", d) for d in (1, 2, 3)]
    bounds = call(
        close_kernel, [shaped(4, SUB, LANE)] * 4, [pltpu.VMEM((4, 4, SUB, LANE), jnp.float32)]
    )(own, snap, c1, *zs, z4, *ys)
    packs = [packs[0]] + [flip(packs[d], "xr", d) for d in (1, 2, 3)]
    turns = []
    for d in TURNS:
        turns.append(call(turn_kernel, shaped(LANE, LANE))(packs[d]))
    bounds = [bounds[0]] + [flip(bounds[d], "xr", d) for d in (1, 2, 3)]
    result = shaped(2, CELLS // 4, 4 * sound_field.shape[2])
    return call(
        cross_kernel,
        result,
        [
            pltpu.VMEM((4, 2, piece, LANE), jnp.float32),
            pltpu.VMEM((4, 3, LANE, LANE), jnp.float32),
            pltpu.VMEM((2, cells, LANE), jnp.float32),
            pltpu.VMEM((cells, LANE), jnp.float32),
            pltpu.VMEM(result.shape, jnp.float32),
            pltpu.SemaphoreType.DMA((8,)),
        ],
        far_out=True,
    )(*bounds, *packs, *turns)


TURNS = (0, 1, 2)


def solution(mesh):
    split = Mesh(mesh.devices.reshape(4, 8, 2, mesh.shape["xr"]), DEPTH + ("xr",))
    in_specs = (P(None, DEPTH, "xr"), P(DEPTH, "xr"), P(DEPTH, "xr"))
    out_specs = P(None, DEPTH + ("xr",), None)

    return jax.shard_map(local, mesh=split, in_specs=in_specs, out_specs=out_specs, check_vma=False)
```

```python
import jax
import jax.numpy as jnp
from jax import lax
from jax.experimental import pallas as pl
from jax.experimental.pallas import tpu as pltpu
from jax.sharding import Mesh
from jax.sharding import PartitionSpec as P

DEPTH = ("y", "z", "c")

DEPTH_STIFFNESS = 1.6
CROSS_STIFFNESS = 1.2
NUMER = complex(2.857, 0.004)
DENOM = complex(2.857, -0.004)

MIX = (NUMER / DENOM) ** 2

SUB = 8
LANE = 128
CELLS = 64
PARTS = 12


def constants(stiffness):
    slope = -0.5 / stiffness
    base = 2.0 - (1.0 / DENOM).real / stiffness - slope
    swing = -(1.0 / DENOM).imag / stiffness
    push = ((DENOM - NUMER) / (NUMER * DENOM * stiffness)).imag
    return base, slope, swing, push


def mul(a, b):
    return a[0] * b[0] - a[1] * b[1], a[0] * b[1] + a[1] * b[0]


def add(a, b):
    return a[0] + b[0], a[1] + b[1]


def sub(a, b):
    return a[0] - b[0], a[1] - b[1]


def scaled(a, s):
    return a[0] * s, a[1] * s


def pick(flag, yes, no):
    return [(jnp.where(flag, p[0], q[0]), jnp.where(flag, p[1], q[1])) for p, q in zip(yes, no)]


def compose(early, late):
    a00, a10, a01, a11, r0, r1 = early
    b00, b10, b01, b11, s0, s1 = late
    return [
        add(mul(b00, a00), mul(b01, a10)),
        add(mul(b10, a00), mul(b11, a10)),
        add(mul(b00, a01), mul(b01, a11)),
        add(mul(b10, a01), mul(b11, a11)),
        add(r0, add(mul(a00, s0), mul(a10, s1))),
        add(r1, add(mul(a01, s0), mul(a11, s1))),
    ]


def normal(state):
    f0, f1, g = state
    size = jnp.maximum(
        jnp.maximum(jnp.abs(f0[0]), jnp.abs(f0[1])), jnp.maximum(jnp.abs(f1[0]), jnp.abs(f1[1]))
    )
    scale = 1.0 / size
    return [scaled(f0, scale), scaled(f1, scale), scaled(g, scale)]


def advance(state, span):
    f0, f1, g = state
    t00, t10, t01, t11, s0, s1 = span
    return [
        add(mul(t00, f0), mul(t01, f1)),
        add(mul(t10, f0), mul(t11, f1)),
        add(g, add(mul(f0, s0), mul(f1, s1))),
    ]


def retreat(state, span):
    p0, p1, h = state
    t00, t10, t01, t11, s0, s1 = span
    q0 = sub(mul(t11, p0), mul(t01, p1))
    q1 = sub(mul(t00, p1), mul(t10, p0))
    return [q0, q1, add(h, add(mul(q0, s0), mul(q1, s1)))]


def meet(left, right):
    f0, f1, g = left
    p0, p1, h = right
    det = sub(mul(f1, p0), mul(f0, p1))
    scale = -1.0 / (det[0] * det[0] + det[1] * det[1])
    inverse = (det[0] * scale, -det[1] * scale)
    v0 = mul(add(mul(f0, h), mul(p0, g)), inverse)
    v1 = mul(add(mul(g, p1), mul(f1, h)), inverse)
    return v0, v1


def ends(like):
    zero = jnp.zeros_like(like)
    one = zero + 1.0
    return [(zero, zero), (one, zero), (zero, zero)], [(one, zero), (zero, zero), (zero, zero)]


def read(ref):
    return [(ref[2 * i], ref[2 * i + 1]) for i in range(PARTS // 2)]


def write(ref, span):
    for i, part in enumerate(span):
        ref[2 * i] = part[0]
        ref[2 * i + 1] = part[1]


def rows(k):
    return pl.ds(SUB * k, SUB)


def step(c, swing, now, past, u=None):
    if u is not None:
        past = sub(past, u)
    return (c * now[0] - (swing * now[1] + past[0]), c * now[1] + (swing * now[0] - past[1]))


def start_pair():
    zero = jnp.zeros((SUB, LANE), jnp.float32)
    one = zero + 1.0
    return [[(one, zero), (zero, zero)], [(zero, zero), (one, zero)]]


def still():
    zero = jnp.zeros((SUB, LANE), jnp.float32)
    return [(zero, zero), (zero, zero)]


def through(matrix, v0, v1):
    t00, t10, t01, t11 = matrix
    return add(mul(t00, v0), mul(t01, v1)), add(mul(t10, v0), mul(t11, v1))


def product(late, early):
    first = through(late, early[0], early[1])
    second = through(late, early[2], early[3])
    return [first[0], first[1], second[0], second[1]]


def sums_of(matrix, p0, p1):
    t00, t10, t01, t11 = matrix
    return sub(mul(t00, p1), mul(t10, p0)), sub(mul(t01, p1), mul(t11, p0))


def read_all(ref, first, count):
    return [(ref[first + 2 * i], ref[first + 2 * i + 1]) for i in range(count)]


def write_all(ref, first, parts):
    for i, part in enumerate(parts):
        ref[first + 2 * i] = part[0]
        ref[first + 2 * i + 1] = part[1]


def open_kernel(field, start, end, own, snap, source, curve, end_in, field_in, start_in, sems):
    base, slope, swing, _ = constants(DEPTH_STIFFNESS)
    loads = [
        pltpu.make_async_copy(a, b, sems.at[i])
        for i, (a, b) in enumerate(((start, start_in), (field, field_in), (end, end_in)))
    ]
    for load in loads:
        load.start()
    tiles = field.shape[2] // LANE
    zero = jnp.zeros((CELLS, LANE), jnp.float32)
    for t in range(tiles, SUB):
        spread = pl.ds(t, CELLS, stride=SUB)
        source[0, spread, :] = zero
        source[1, spread, :] = zero
        curve[spread, :] = zero + (base + 0.9 * slope)
    loads[0].wait()
    for t in range(tiles):
        spread, cols = pl.ds(t, CELLS, stride=SUB), slice(t * LANE, (t + 1) * LANE)
        curve[spread, :] = base + slope * start_in[:, cols]
    loads[1].wait()
    for t in range(tiles):
        spread, cols = pl.ds(t, CELLS, stride=SUB), slice(t * LANE, (t + 1) * LANE)
        source[0, spread, :] = field_in[0, :, cols]
        source[1, spread, :] = field_in[1, :, cols]
    waves = start_pair()
    march = still()
    for k in range(CELLS):
        u, c = (source[0, rows(k), :], source[1, rows(k), :]), curve[rows(k), :]
        march = [march[1], step(c, swing, march[1], march[0], u)]
        waves = [[w[1], step(c, swing, w[1], w[0])] for w in waves]
        if k % (CELLS // 4) == CELLS // 4 - 1 and k < CELLS - 1:
            write(snap.at[k // (CELLS // 4)], waves[0] + waves[1] + march)
    matrix = waves[0] + waves[1]
    write(own, matrix + list(sums_of(matrix, *march)))
    loads[2].wait()


def stow_kernel(source, curve, end, *packs):
    xbase, xslope, _, _ = constants(CROSS_STIFFNESS)
    tiles = end.shape[1] // LANE
    x = lax.axis_index("xr")
    count = CELLS // 4
    for d, pack in enumerate(packs):
        here = pl.ds(pl.multiple_of((x ^ d) * SUB * count, SUB * count), SUB * count)
        re, im = source[0, here, :], source[1, here, :]
        pack[0] = MIX.real * re - MIX.imag * im
        pack[1] = MIX.real * im + MIX.imag * re
        pack[2] = curve[here, :]
        first = pl.multiple_of((x ^ d) * count, count)
        for t in range(tiles):
            cols = slice(t * LANE, (t + 1) * LANE)
            pack[3, pl.ds(t, count, stride=SUB), :] = xbase + xslope * end[pl.ds(first, count), cols]
        for t in range(tiles, SUB):
            pack[3, pl.ds(t, count, stride=SUB), :] = jnp.zeros((count, LANE), jnp.float32) + (
                xbase + 0.9 * xslope
            )


def turn_kernel(pack, turned):
    turned[...] = pack[3].T


def pair_kernel(axis, bit, own, other, total):
    upper = ((lax.axis_index(axis) >> bit) & 1) == 1
    a, b = read(own), read(other)
    write(total, compose(pick(upper, b, a), pick(upper, a, b)))


def quad_kernel(axis, own, other1, other2, other3, total):
    place = lax.axis_index(axis)
    odd = (place & 1) == 1
    high = (place & 2) == 2
    a, r1, r2, r3 = read(own), read(other1), read(other2), read(other3)
    mine = compose(pick(odd, r1, a), pick(odd, a, r1))
    theirs = compose(pick(odd, r3, r2), pick(odd, r2, r3))
    write(total, compose(pick(high, theirs, mine), pick(high, mine, theirs)))


def descend_pair(left, right, upper, other):
    return (
        pick(upper, normal(advance(left, other)), left),
        pick(upper, right, normal(retreat(right, other))),
    )


def descend_quad(left, right, place, r1, r2, r3):
    odd = (place & 1) == 1
    high = (place & 2) == 2
    first, second = pick(odd, r3, r2), pick(odd, r2, r3)
    left = pick(high, normal(advance(normal(advance(left, first)), second)), left)
    right = pick(high, right, normal(retreat(normal(retreat(right, second)), first)))
    return descend_pair(left, right, odd, r1)


def close_kernel(own, snap, c1, z1, z2, z3, z4, y1, y2, y3, bound0, bound1, bound2, bound3, bounds):
    x, y, z, c = (lax.axis_index(name) for name in ("xr",) + DEPTH)
    left, right = ends(own[0])
    left, right = descend_quad(left, right, y, read(y1), read(y2), read(y3))
    left, right = descend_pair(left, right, (z & 4) == 4, read(z4))
    left, right = descend_quad(left, right, z & 3, read(z1), read(z2), read(z3))
    left, right = descend_pair(left, right, c == 1, read(c1))
    right = normal(retreat(right, read(own)))
    v0, v1 = meet(left, right)
    for i in range(4):
        a, b = v0, v1
        if i:
            span = read(snap.at[i - 1])
            a, b = through(span[:4], v0, v1)
            a, b = add(a, span[4]), add(b, span[5])
        for j, part in enumerate((a, b)):
            bounds[i, 2 * j] = MIX.real * part[0] - MIX.imag * part[1]
            bounds[i, 2 * j + 1] = MIX.real * part[1] + MIX.imag * part[0]
    for d, bound in enumerate((bound0, bound1, bound2, bound3)):
        bound[...] = bounds[x ^ d]


LEVELS = ((0, 1), (1, 1), (1, 2), (1, 4), (0, 2), (0, 4))
HALF = CELLS // 2
LATE, WHOLE, SOLVE, OWN, LEVEL0, PER_LEVEL = 8, 16, 24, 32, 36, 16


def upper_of(axis, stride):
    return (lax.broadcasted_iota(jnp.int32, (SUB, LANE), axis) & stride) == stride


def swapped(v, axis, stride, upper):
    size = SUB if axis == 0 else LANE
    down = pltpu.roll(v, stride, axis)
    if 2 * stride == size:
        return down
    return jnp.where(upper, down, pltpu.roll(v, size - stride, axis))


def swapped_all(parts, axis, stride, upper):
    return [(swapped(p[0], axis, stride, upper), swapped(p[1], axis, stride, upper)) for p in parts]


def plan_kernel(*refs):
    tiles, turns, last, curve, plan, whole = refs[0], refs[1:4], refs[4], refs[5], refs[6], refs[7]
    _, _, swing, _ = constants(CROSS_STIFFNESS)
    x = lax.axis_index("xr")
    for d in range(4):
        whole[x ^ d] = turns[d][...] if d < 3 else last[3].T
    for q in range(4):
        for h in range(2):
            curve[pl.ds(2 * q + h, CELLS, stride=SUB), :] = whole[q, CELLS * h : CELLS * (h + 1), :]
    halves = [start_pair(), start_pair()]
    for k in range(HALF):
        for h in range(2):
            c = curve[rows(k + HALF * h), :]
            halves[h] = [[w[1], step(c, swing, w[1], w[0])] for w in halves[h]]
    early, late = (w[0] + w[1] for w in halves)
    write_all(plan, 0, early)
    write_all(plan, LATE, late)
    matrix = product(late, early)
    write_all(plan, WHOLE, matrix)
    lane = lax.broadcasted_iota(jnp.int32, (SUB, LANE), 1)
    unit = start_pair()
    unit = unit[0] + unit[1]
    matrix = pick((lane & 7) >= tiles, unit, matrix)
    total = matrix
    stages = []
    for i, (axis, stride) in enumerate(LEVELS):
        upper = upper_of(axis, stride)
        other = swapped_all(total, axis, stride, upper)
        low = pick(upper, other, total)
        stages.append((upper, other))
        if i < 5:
            write_all(plan, LEVEL0 + PER_LEVEL * i, low)
            total = product(pick(upper, total, other), low)
    zero = jnp.zeros((SUB, LANE), jnp.float32)
    one = zero + 1.0
    left, right = [(zero, zero), (one, zero)], [(one, zero), (zero, zero)]
    left_weights, right_weights = [], []

    def rescale(pair, weights):
        size = jnp.maximum(
            jnp.maximum(jnp.abs(pair[0][0]), jnp.abs(pair[0][1])),
            jnp.maximum(jnp.abs(pair[1][0]), jnp.abs(pair[1][1])),
        )
        scale = 1.0 / size
        return [scaled(p, scale) for p in pair], [[scaled(w, scale) for w in ws] for ws in weights]

    for upper, other in reversed(stages):
        gone = list(through(other, left[0], left[1]))
        left_weights.append([scaled(p, jnp.where(upper, 1.0, 0.0)) for p in left])
        left, left_weights = rescale(pick(upper, gone, left), left_weights)
        t00, t10, t01, t11 = other
        back = [sub(mul(t11, right[0]), mul(t01, right[1])), sub(mul(t00, right[1]), mul(t10, right[0]))]
        right_weights.append([scaled(p, jnp.where(upper, 0.0, 1.0)) for p in back])
        right, right_weights = rescale(pick(upper, right, back), right_weights)
    t00, t10, t01, t11 = matrix
    right = [sub(mul(t11, right[0]), mul(t01, right[1])), sub(mul(t00, right[1]), mul(t10, right[0]))]
    right_weights.append(right)
    right, right_weights = rescale(right, right_weights)
    det = sub(mul(left[1], right[0]), mul(left[0], right[1]))
    scale = -1.0 / (det[0] * det[0] + det[1] * det[1])
    inverse = (det[0] * scale, -det[1] * scale)
    write_all(plan, SOLVE, [mul(p, inverse) for p in (left[0], right[0], right[1], left[1])])
    write_all(plan, OWN, right_weights[-1])
    for i in range(6):
        write_all(plan, LEVEL0 + PER_LEVEL * i + 8, left_weights[5 - i] + right_weights[5 - i])


def cross_kernel(*refs):
    bounds, packs, curve, plan, (result, mid, turned, source, out, sems) = (
        refs[:4], refs[4:8], refs[8], refs[9], refs[10:],
    )
    _, _, swing, push = constants(DEPTH_STIFFNESS)
    tiles = result.shape[2] // LANE // 4
    x = lax.axis_index("xr")
    lines = CELLS // 4
    for d in range(4):
        pack, bound = packs[d], bounds[d]
        past, now = (bound[0], bound[1]), (bound[2], bound[3])
        for k in range(lines):
            u, c = (pack[0, rows(k), :], pack[1, rows(k), :]), pack[2, rows(k), :]
            mid[d, 0, rows(k), :] = u[0] - push * now[1]
            mid[d, 1, rows(k), :] = u[1] + push * now[0]
            past, now = now, step(c, swing, now, past, u)
        at = x ^ d
        turned[at, 0] = mid[d, 0].T
        turned[at, 1] = mid[d, 1].T
    _, _, swing, push = constants(CROSS_STIFFNESS)
    for q in range(4):
        for h in range(2):
            spread = pl.ds(2 * q + h, CELLS, stride=SUB)
            half = slice(CELLS * h, CELLS * (h + 1))
            source[0, spread, :] = turned[q, 0, half, :]
            source[1, spread, :] = turned[q, 1, half, :]

    def cell(k):
        return (source[0, rows(k), :], source[1, rows(k), :]), curve[rows(k), :]

    marches = [still(), still()]
    for k in range(HALF):
        for h in range(2):
            u, c = cell(k + HALF * h)
            past, now = marches[h]
            marches[h] = [now, step(c, swing, now, past, u)]
    early, late, matrix = (read_all(plan, first, 4) for first in (0, LATE, WHOLE))
    end0, end1 = through(late, *marches[0])
    end0, end1 = add(end0, marches[1][0]), add(end1, marches[1][1])
    valid = (lax.broadcasted_iota(jnp.int32, (SUB, LANE), 1) & 7) < tiles
    zero = jnp.zeros((SUB, LANE), jnp.float32)
    sums = [(jnp.where(valid, s[0], zero), jnp.where(valid, s[1], zero)) for s in sums_of(matrix, end0, end1)]
    w0, w1 = read_all(plan, OWN, 2)
    g, h = (zero, zero), add(mul(w0, sums[0]), mul(w1, sums[1]))
    for i, (axis, stride) in enumerate(LEVELS):
        upper = upper_of(axis, stride)
        other = swapped_all(sums, axis, stride, upper)
        l0, l1, r0, r1 = read_all(plan, LEVEL0 + PER_LEVEL * i + 8, 4)
        g = add(g, add(mul(l0, other[0]), mul(l1, other[1])))
        h = add(h, add(mul(r0, other[0]), mul(r1, other[1])))
        if i < 5:
            t00, t10, t01, t11 = read_all(plan, LEVEL0 + PER_LEVEL * i, 4)
            low, high = pick(upper, other, sums), pick(upper, sums, other)
            sums = [
                add(low[0], add(mul(t00, high[0]), mul(t10, high[1]))),
                add(low[1], add(mul(t01, high[0]), mul(t11, high[1]))),
            ]
    f0, p0, p1, f1 = read_all(plan, SOLVE, 4)
    v0 = add(mul(f0, h), mul(p0, g))
    v1 = add(mul(p1, g), mul(f1, h))
    half = through(early, v0, v1)
    states = [[v0, v1], [add(half[0], marches[0][0]), add(half[1], marches[0][1])]]
    for k in range(HALF):
        for h in range(2):
            u, c = cell(k + HALF * h)
            past, now = states[h]
            source[0, rows(k + HALF * h), :] = u[0] - push * now[1]
            source[1, rows(k + HALF * h), :] = u[1] + push * now[0]
            states[h] = [now, step(c, swing, now, past, u)]
    stores = []
    for q in range(4):
        for part in range(2):
            halves = [source[part, pl.ds(2 * q + h, CELLS, stride=SUB), :] for h in range(2)]
            turned[q, part] = jnp.concatenate(halves, axis=0).T
            for t in range(tiles):
                cols = slice((q * tiles + t) * LANE, (q * tiles + t + 1) * LANE)
                out[part, :, cols] = turned[q, part, pl.ds(t, lines, stride=SUB), :]
            whole = pl.ds(q * tiles * LANE, tiles * LANE)
            store = pltpu.make_async_copy(
                out.at[part, :, whole], result.at[part, :, whole], sems.at[4 * part + q]
            )
            store.start()
            stores.append(store)
    for store in stores:
        store.wait()


def shaped(*shape):
    return jax.ShapeDtypeStruct(shape, jnp.float32)


def call(kernel, outs, scratch=(), far_in=False, far_out=False):
    far, here = pl.BlockSpec(memory_space=pltpu.HBM), pl.BlockSpec(memory_space=pltpu.VMEM)
    out_specs = [far if far_out else here] * len(outs) if isinstance(outs, list) else (far if far_out else here)

    def run(*values):
        return pl.pallas_call(
            kernel,
            out_shape=outs,
            in_specs=[far if far_in else here] * len(values),
            out_specs=out_specs,
            scratch_shapes=list(scratch),
            compiler_params=pltpu.CompilerParams(vmem_limit_bytes=8 << 20),
            cost_estimate=pl.CostEstimate(flops=100000, bytes_accessed=1000000, transcendentals=0),
        )(*values)

    return run


def local(sound_field, index_start, index_end):
    span_shape = shaped(PARTS, SUB, LANE)
    cells = SUB * CELLS
    piece = cells // 4
    inputs = (sound_field, index_start, index_end)
    own, snap, source, curve, end = call(
        open_kernel,
        [
            span_shape,
            shaped(3, PARTS, SUB, LANE),
            shaped(2, cells, LANE),
            shaped(cells, LANE),
            shaped(*index_end.shape),
        ],
        [pltpu.VMEM(v.shape, jnp.float32) for v in inputs[:2]] + [pltpu.SemaphoreType.DMA((3,))],
        far_in=True,
    )(*(pltpu.with_memory_space_constraint(v, pltpu.HBM) for v in inputs))
    packs = call(stow_kernel, [shaped(4, piece, LANE)] * 4)(source, curve, end)

    def flip(value, axis, d):
        return lax.ppermute(value, axis, [(i, i ^ d) for i in range(lax.axis_size(axis))])

    def pair(axis, bit, a, b):
        return call(lambda *refs: pair_kernel(axis, bit, *refs), span_shape)(a, b)

    def quad(axis, a, others):
        return call(lambda *refs: quad_kernel(axis, *refs), span_shape)(a, *others)

    c1 = flip(own, "c", 1)
    total = pair("c", 0, own, c1)
    zs = [flip(total, "z", d) for d in (1, 2, 3)]
    total = quad("z", total, zs)
    z4 = lax.ppermute(total, "z", [(i, 7 - i) for i in range(8)])
    total = pair("z", 2, total, z4)
    ys = [flip(total, "y", d) for d in (1, 2, 3)]
    bounds = call(
        close_kernel, [shaped(4, SUB, LANE)] * 4, [pltpu.VMEM((4, 4, SUB, LANE), jnp.float32)]
    )(own, snap, c1, *zs, z4, *ys)
    packs = [packs[0]] + [flip(packs[d], "xr", d) for d in (1, 2, 3)]
    turns = []
    for d in TURNS:
        turns.append(call(turn_kernel, shaped(LANE, LANE))(packs[d]))
    bounds = [bounds[0]] + [flip(bounds[d], "xr", d) for d in (1, 2, 3)]
    tiles = sound_field.shape[2] // LANE
    curve, plan = call(
        lambda *refs: plan_kernel(tiles, *refs),
        [shaped(cells, LANE), shaped(LEVEL0 + 6 * PER_LEVEL, SUB, LANE)],
        [pltpu.VMEM((4, LANE, LANE), jnp.float32)],
    )(*turns, packs[3])
    result = shaped(2, CELLS // 4, 4 * sound_field.shape[2])
    return call(
        cross_kernel,
        result,
        [
            pltpu.VMEM((4, 2, piece, LANE), jnp.float32),
            pltpu.VMEM((4, 2, LANE, LANE), jnp.float32),
            pltpu.VMEM((2, cells, LANE), jnp.float32),
            pltpu.VMEM(result.shape, jnp.float32),
            pltpu.SemaphoreType.DMA((8,)),
        ],
        far_out=True,
    )(*bounds, *packs, curve, plan)


TURNS = (0, 1, 2)


def solution(mesh):
    split = Mesh(mesh.devices.reshape(4, 8, 2, mesh.shape["xr"]), DEPTH + ("xr",))
    in_specs = (P(None, DEPTH, "xr"), P(DEPTH, "xr"), P(DEPTH, "xr"))
    out_specs = P(None, DEPTH + ("xr",), None)

    return jax.shard_map(local, mesh=split, in_specs=in_specs, out_specs=out_specs, check_vma=False)
```

```python
import jax
import jax.numpy as jnp
from jax import lax
from jax.experimental import pallas as pl
from jax.experimental.pallas import tpu as pltpu
from jax.sharding import Mesh
from jax.sharding import PartitionSpec as P

DEPTH = ("y", "z", "c")

DEPTH_STIFFNESS = 1.6
CROSS_STIFFNESS = 1.2
NUMER = complex(2.857, 0.004)
DENOM = complex(2.857, -0.004)

MIX = (NUMER / DENOM) ** 2

SUB = 8
LANE = 128
CELLS = 64
PARTS = 12


def constants(stiffness):
    slope = -0.5 / stiffness
    base = 2.0 - (1.0 / DENOM).real / stiffness - slope
    swing = -(1.0 / DENOM).imag / stiffness
    push = ((DENOM - NUMER) / (NUMER * DENOM * stiffness)).imag
    return base, slope, swing, push


def mul(a, b):
    return a[0] * b[0] - a[1] * b[1], a[0] * b[1] + a[1] * b[0]


def add(a, b):
    return a[0] + b[0], a[1] + b[1]


def sub(a, b):
    return a[0] - b[0], a[1] - b[1]


def scaled(a, s):
    return a[0] * s, a[1] * s


def pick(flag, yes, no):
    return [(jnp.where(flag, p[0], q[0]), jnp.where(flag, p[1], q[1])) for p, q in zip(yes, no)]


def compose(early, late):
    a00, a10, a01, a11, r0, r1 = early
    b00, b10, b01, b11, s0, s1 = late
    return [
        add(mul(b00, a00), mul(b01, a10)),
        add(mul(b10, a00), mul(b11, a10)),
        add(mul(b00, a01), mul(b01, a11)),
        add(mul(b10, a01), mul(b11, a11)),
        add(r0, add(mul(a00, s0), mul(a10, s1))),
        add(r1, add(mul(a01, s0), mul(a11, s1))),
    ]


def normal(state):
    f0, f1, g = state
    size = jnp.maximum(
        jnp.maximum(jnp.abs(f0[0]), jnp.abs(f0[1])), jnp.maximum(jnp.abs(f1[0]), jnp.abs(f1[1]))
    )
    scale = 1.0 / size
    return [scaled(f0, scale), scaled(f1, scale), scaled(g, scale)]


def advance(state, span):
    f0, f1, g = state
    t00, t10, t01, t11, s0, s1 = span
    return [
        add(mul(t00, f0), mul(t01, f1)),
        add(mul(t10, f0), mul(t11, f1)),
        add(g, add(mul(f0, s0), mul(f1, s1))),
    ]


def retreat(state, span):
    p0, p1, h = state
    t00, t10, t01, t11, s0, s1 = span
    q0 = sub(mul(t11, p0), mul(t01, p1))
    q1 = sub(mul(t00, p1), mul(t10, p0))
    return [q0, q1, add(h, add(mul(q0, s0), mul(q1, s1)))]


def meet(left, right):
    f0, f1, g = left
    p0, p1, h = right
    det = sub(mul(f1, p0), mul(f0, p1))
    scale = -1.0 / (det[0] * det[0] + det[1] * det[1])
    inverse = (det[0] * scale, -det[1] * scale)
    v0 = mul(add(mul(f0, h), mul(p0, g)), inverse)
    v1 = mul(add(mul(g, p1), mul(f1, h)), inverse)
    return v0, v1


def ends(like):
    zero = jnp.zeros_like(like)
    one = zero + 1.0
    return [(zero, zero), (one, zero), (zero, zero)], [(one, zero), (zero, zero), (zero, zero)]


SPREAD = 7


def read(ref):
    values = [ref[SUB * i : SUB * (i + 1), :] for i in range(9)] + [ref[pl.ds(SPREAD, SUB, stride=SUB), :]]
    t00, t10, along, s0, s1 = zip(values[0::2], values[1::2])
    scale = 1.0 / (t00[0] * t00[0] + t00[1] * t00[1] + t10[0] * t10[0] + t10[1] * t10[1])
    p, q = mul(along, t00), mul(along, t10)
    t01 = (p[0] - t10[0] * scale, p[1] + t10[1] * scale)
    t11 = (q[0] + t00[0] * scale, q[1] - t00[1] * scale)
    return [t00, t10, t01, t11, s0, s1]


def write(ref, span):
    t00, t10, t01, t11, s0, s1 = span
    scale = 1.0 / (t00[0] * t00[0] + t00[1] * t00[1] + t10[0] * t10[0] + t10[1] * t10[1])
    along = add(mul((t00[0], -t00[1]), t01), mul((t10[0], -t10[1]), t11))
    values = [*t00, *t10, *scaled(along, scale), *s0, *s1]
    for i in range(9):
        ref[SUB * i : SUB * (i + 1), :] = values[i]
    ref[pl.ds(SPREAD, SPREAD, stride=SUB), :] = values[9][:SPREAD]


def rows(k):
    return pl.ds(SUB * k, SUB)


def step(c, swing, now, past, u=None):
    if u is not None:
        past = sub(past, u)
    return (c * now[0] - (swing * now[1] + past[0]), c * now[1] + (swing * now[0] - past[1]))


def start_pair():
    zero = jnp.zeros((SUB, LANE), jnp.float32)
    one = zero + 1.0
    return [[(one, zero), (zero, zero)], [(zero, zero), (one, zero)]]


def still():
    zero = jnp.zeros((SUB, LANE), jnp.float32)
    return [(zero, zero), (zero, zero)]


def through(matrix, v0, v1):
    t00, t10, t01, t11 = matrix
    return add(mul(t00, v0), mul(t01, v1)), add(mul(t10, v0), mul(t11, v1))


def product(late, early):
    first = through(late, early[0], early[1])
    second = through(late, early[2], early[3])
    return [first[0], first[1], second[0], second[1]]


def sums_of(matrix, p0, p1):
    t00, t10, t01, t11 = matrix
    return sub(mul(t00, p1), mul(t10, p0)), sub(mul(t01, p1), mul(t11, p0))


def read_all(ref, first, count):
    return [(ref[first + 2 * i], ref[first + 2 * i + 1]) for i in range(count)]


def write_all(ref, first, parts):
    for i, part in enumerate(parts):
        ref[first + 2 * i] = part[0]
        ref[first + 2 * i + 1] = part[1]


def open_kernel(field, start, end, own, snap, source, curve, end_in, field_in, start_in, sems):
    base, slope, swing, _ = constants(DEPTH_STIFFNESS)
    loads = [
        pltpu.make_async_copy(a, b, sems.at[i])
        for i, (a, b) in enumerate(((start, start_in), (field, field_in), (end, end_in)))
    ]
    for load in loads:
        load.start()
    tiles = field.shape[2] // LANE
    zero = jnp.zeros((CELLS, LANE), jnp.float32)
    for t in range(tiles, SUB):
        spread = pl.ds(t, CELLS, stride=SUB)
        source[0, spread, :] = zero
        source[1, spread, :] = zero
        curve[spread, :] = zero + (base + 0.9 * slope)
    loads[0].wait()
    for t in range(tiles):
        spread, cols = pl.ds(t, CELLS, stride=SUB), slice(t * LANE, (t + 1) * LANE)
        curve[spread, :] = base + slope * start_in[:, cols]
    loads[1].wait()
    for t in range(tiles):
        spread, cols = pl.ds(t, CELLS, stride=SUB), slice(t * LANE, (t + 1) * LANE)
        source[0, spread, :] = field_in[0, :, cols]
        source[1, spread, :] = field_in[1, :, cols]
    waves = start_pair()
    march = still()
    for k in range(CELLS):
        u, c = (source[0, rows(k), :], source[1, rows(k), :]), curve[rows(k), :]
        march = [march[1], step(c, swing, march[1], march[0], u)]
        waves = [[w[1], step(c, swing, w[1], w[0])] for w in waves]
        if k % (CELLS // 4) == CELLS // 4 - 1 and k < CELLS - 1:
            write_all(snap.at[k // (CELLS // 4)], 0, waves[0] + waves[1] + march)
    matrix = waves[0] + waves[1]
    write(own, matrix + list(sums_of(matrix, *march)))
    loads[2].wait()


def stow_kernel(source, curve, end, *packs):
    xbase, xslope, _, _ = constants(CROSS_STIFFNESS)
    tiles = end.shape[1] // LANE
    x = lax.axis_index("xr")
    count = CELLS // 4
    for d, pack in enumerate(packs):
        here = pl.ds(pl.multiple_of((x ^ d) * SUB * count, SUB * count), SUB * count)
        re, im = source[0, here, :], source[1, here, :]
        pack[0] = MIX.real * re - MIX.imag * im
        pack[1] = MIX.real * im + MIX.imag * re
        pack[2] = curve[here, :]
        first = pl.multiple_of((x ^ d) * count, count)
        for t in range(tiles):
            cols = slice(t * LANE, (t + 1) * LANE)
            pack[3, pl.ds(t, count, stride=SUB), :] = xbase + xslope * end[pl.ds(first, count), cols]
        for t in range(tiles, SUB):
            pack[3, pl.ds(t, count, stride=SUB), :] = jnp.zeros((count, LANE), jnp.float32) + (
                xbase + 0.9 * xslope
            )


def turn_kernel(pack, turned):
    turned[...] = pack[3].T


def pair_kernel(axis, bit, own, other, total):
    upper = ((lax.axis_index(axis) >> bit) & 1) == 1
    a, b = read(own), read(other)
    write(total, compose(pick(upper, b, a), pick(upper, a, b)))


def quad_kernel(axis, own, other1, other2, other3, total):
    place = lax.axis_index(axis)
    odd = (place & 1) == 1
    high = (place & 2) == 2
    a, r1, r2, r3 = read(own), read(other1), read(other2), read(other3)
    mine = compose(pick(odd, r1, a), pick(odd, a, r1))
    theirs = compose(pick(odd, r3, r2), pick(odd, r2, r3))
    write(total, compose(pick(high, theirs, mine), pick(high, mine, theirs)))


def descend_pair(left, right, upper, other):
    return (
        pick(upper, normal(advance(left, other)), left),
        pick(upper, right, normal(retreat(right, other))),
    )


def descend_quad(left, right, place, r1, r2, r3):
    odd = (place & 1) == 1
    high = (place & 2) == 2
    first, second = pick(odd, r3, r2), pick(odd, r2, r3)
    left = pick(high, normal(advance(normal(advance(left, first)), second)), left)
    right = pick(high, right, normal(retreat(normal(retreat(right, second)), first)))
    return descend_pair(left, right, odd, r1)


def close_kernel(own, snap, c1, z1, z2, z3, z4, y1, y2, y3, bound0, bound1, bound2, bound3, bounds):
    x, y, z, c = (lax.axis_index(name) for name in ("xr",) + DEPTH)
    left, right = ends(snap[0, 0])
    left, right = descend_quad(left, right, y, read(y1), read(y2), read(y3))
    left, right = descend_pair(left, right, (z & 4) == 4, read(z4))
    left, right = descend_quad(left, right, z & 3, read(z1), read(z2), read(z3))
    left, right = descend_pair(left, right, c == 1, read(c1))
    right = normal(retreat(right, read(own)))
    v0, v1 = meet(left, right)
    used = lax.broadcasted_iota(jnp.int32, (SUB, LANE), 0) < SPREAD
    for i in range(4):
        a, b = v0, v1
        if i:
            span = read_all(snap.at[i - 1], 0, 6)
            a, b = through(span[:4], v0, v1)
            a, b = add(a, span[4]), add(b, span[5])
        for j, part in enumerate((a, b)):
            bounds[i, 2 * j] = jnp.where(used, MIX.real * part[0] - MIX.imag * part[1], 0.0)
            bounds[i, 2 * j + 1] = jnp.where(used, MIX.real * part[1] + MIX.imag * part[0], 0.0)
    for d, bound in enumerate((bound0, bound1, bound2, bound3)):
        bound[...] = bounds[x ^ d]


LEVELS = ((0, 1), (1, 1), (1, 2), (1, 4), (0, 2), (0, 4))
HALF = CELLS // 2
LATE, WHOLE, SOLVE, OWN, LEVEL0, PER_LEVEL = 8, 16, 24, 32, 36, 16


def upper_of(axis, stride):
    return (lax.broadcasted_iota(jnp.int32, (SUB, LANE), axis) & stride) == stride


def swapped(v, axis, stride, upper):
    size = SUB if axis == 0 else LANE
    down = pltpu.roll(v, stride, axis)
    if 2 * stride == size:
        return down
    return jnp.where(upper, down, pltpu.roll(v, size - stride, axis))


def swapped_all(parts, axis, stride, upper):
    return [(swapped(p[0], axis, stride, upper), swapped(p[1], axis, stride, upper)) for p in parts]


def plan_kernel(*refs):
    tiles, turns, last, curve, plan, whole = refs[0], refs[1:4], refs[4], refs[5], refs[6], refs[7]
    _, _, swing, _ = constants(CROSS_STIFFNESS)
    x = lax.axis_index("xr")
    for d in range(4):
        whole[x ^ d] = turns[d][...] if d < 3 else last[3].T
    for q in range(4):
        for h in range(2):
            curve[pl.ds(2 * q + h, CELLS, stride=SUB), :] = whole[q, CELLS * h : CELLS * (h + 1), :]
    halves = [start_pair(), start_pair()]
    for k in range(HALF):
        for h in range(2):
            c = curve[rows(k + HALF * h), :]
            halves[h] = [[w[1], step(c, swing, w[1], w[0])] for w in halves[h]]
    early, late = (w[0] + w[1] for w in halves)
    write_all(plan, 0, early)
    write_all(plan, LATE, late)
    matrix = product(late, early)
    write_all(plan, WHOLE, matrix)
    lane = lax.broadcasted_iota(jnp.int32, (SUB, LANE), 1)
    unit = start_pair()
    unit = unit[0] + unit[1]
    matrix = pick((lane & 7) >= tiles, unit, matrix)
    total = matrix
    stages = []
    for i, (axis, stride) in enumerate(LEVELS):
        upper = upper_of(axis, stride)
        other = swapped_all(total, axis, stride, upper)
        low = pick(upper, other, total)
        stages.append((upper, other))
        if i < 5:
            write_all(plan, LEVEL0 + PER_LEVEL * i, low)
            total = product(pick(upper, total, other), low)
    zero = jnp.zeros((SUB, LANE), jnp.float32)
    one = zero + 1.0
    left, right = [(zero, zero), (one, zero)], [(one, zero), (zero, zero)]
    left_weights, right_weights = [], []

    def rescale(pair, weights):
        size = jnp.maximum(
            jnp.maximum(jnp.abs(pair[0][0]), jnp.abs(pair[0][1])),
            jnp.maximum(jnp.abs(pair[1][0]), jnp.abs(pair[1][1])),
        )
        scale = 1.0 / size
        return [scaled(p, scale) for p in pair], [[scaled(w, scale) for w in ws] for ws in weights]

    for upper, other in reversed(stages):
        gone = list(through(other, left[0], left[1]))
        left_weights.append([scaled(p, jnp.where(upper, 1.0, 0.0)) for p in left])
        left, left_weights = rescale(pick(upper, gone, left), left_weights)
        t00, t10, t01, t11 = other
        back = [sub(mul(t11, right[0]), mul(t01, right[1])), sub(mul(t00, right[1]), mul(t10, right[0]))]
        right_weights.append([scaled(p, jnp.where(upper, 0.0, 1.0)) for p in back])
        right, right_weights = rescale(pick(upper, right, back), right_weights)
    t00, t10, t01, t11 = matrix
    right = [sub(mul(t11, right[0]), mul(t01, right[1])), sub(mul(t00, right[1]), mul(t10, right[0]))]
    right_weights.append(right)
    right, right_weights = rescale(right, right_weights)
    det = sub(mul(left[1], right[0]), mul(left[0], right[1]))
    scale = -1.0 / (det[0] * det[0] + det[1] * det[1])
    inverse = (det[0] * scale, -det[1] * scale)
    write_all(plan, SOLVE, [mul(p, inverse) for p in (left[0], right[0], right[1], left[1])])
    write_all(plan, OWN, right_weights[-1])
    for i in range(6):
        write_all(plan, LEVEL0 + PER_LEVEL * i + 8, left_weights[5 - i] + right_weights[5 - i])


def cross_kernel(*refs):
    bounds, packs, curve, plan, (result, mid, turned, source, out, sems) = (
        refs[:4], refs[4:8], refs[8], refs[9], refs[10:],
    )
    _, _, swing, push = constants(DEPTH_STIFFNESS)
    tiles = result.shape[2] // LANE // 4
    x = lax.axis_index("xr")
    lines = CELLS // 4
    for d in range(4):
        pack, bound = packs[d], bounds[d]
        past, now = (bound[0], bound[1]), (bound[2], bound[3])
        for k in range(lines):
            u, c = (pack[0, rows(k), :], pack[1, rows(k), :]), pack[2, rows(k), :]
            mid[d, 0, rows(k), :] = u[0] - push * now[1]
            mid[d, 1, rows(k), :] = u[1] + push * now[0]
            past, now = now, step(c, swing, now, past, u)
        at = x ^ d
        turned[at, 0] = mid[d, 0].T
        turned[at, 1] = mid[d, 1].T
    _, _, swing, push = constants(CROSS_STIFFNESS)
    for q in range(4):
        for h in range(2):
            spread = pl.ds(2 * q + h, CELLS, stride=SUB)
            half = slice(CELLS * h, CELLS * (h + 1))
            source[0, spread, :] = turned[q, 0, half, :]
            source[1, spread, :] = turned[q, 1, half, :]

    def cell(k):
        return (source[0, rows(k), :], source[1, rows(k), :]), curve[rows(k), :]

    marches = [still(), still()]
    for k in range(HALF):
        for h in range(2):
            u, c = cell(k + HALF * h)
            past, now = marches[h]
            marches[h] = [now, step(c, swing, now, past, u)]
    early, late, matrix = (read_all(plan, first, 4) for first in (0, LATE, WHOLE))
    end0, end1 = through(late, *marches[0])
    end0, end1 = add(end0, marches[1][0]), add(end1, marches[1][1])
    valid = (lax.broadcasted_iota(jnp.int32, (SUB, LANE), 1) & 7) < tiles
    zero = jnp.zeros((SUB, LANE), jnp.float32)
    sums = [(jnp.where(valid, s[0], zero), jnp.where(valid, s[1], zero)) for s in sums_of(matrix, end0, end1)]
    w0, w1 = read_all(plan, OWN, 2)
    g, h = (zero, zero), add(mul(w0, sums[0]), mul(w1, sums[1]))
    for i, (axis, stride) in enumerate(LEVELS):
        upper = upper_of(axis, stride)
        other = swapped_all(sums, axis, stride, upper)
        l0, l1, r0, r1 = read_all(plan, LEVEL0 + PER_LEVEL * i + 8, 4)
        g = add(g, add(mul(l0, other[0]), mul(l1, other[1])))
        h = add(h, add(mul(r0, other[0]), mul(r1, other[1])))
        if i < 5:
            t00, t10, t01, t11 = read_all(plan, LEVEL0 + PER_LEVEL * i, 4)
            low, high = pick(upper, other, sums), pick(upper, sums, other)
            sums = [
                add(low[0], add(mul(t00, high[0]), mul(t10, high[1]))),
                add(low[1], add(mul(t01, high[0]), mul(t11, high[1]))),
            ]
    f0, p0, p1, f1 = read_all(plan, SOLVE, 4)
    v0 = add(mul(f0, h), mul(p0, g))
    v1 = add(mul(p1, g), mul(f1, h))
    half = through(early, v0, v1)
    states = [[v0, v1], [add(half[0], marches[0][0]), add(half[1], marches[0][1])]]
    for k in range(HALF):
        for h in range(2):
            u, c = cell(k + HALF * h)
            past, now = states[h]
            source[0, rows(k + HALF * h), :] = u[0] - push * now[1]
            source[1, rows(k + HALF * h), :] = u[1] + push * now[0]
            states[h] = [now, step(c, swing, now, past, u)]
    stores = []
    for q in range(4):
        for part in range(2):
            halves = [source[part, pl.ds(2 * q + h, CELLS, stride=SUB), :] for h in range(2)]
            turned[q, part] = jnp.concatenate(halves, axis=0).T
            for t in range(tiles):
                cols = slice((q * tiles + t) * LANE, (q * tiles + t + 1) * LANE)
                out[part, :, cols] = turned[q, part, pl.ds(t, lines, stride=SUB), :]
            whole = pl.ds(q * tiles * LANE, tiles * LANE)
            store = pltpu.make_async_copy(
                out.at[part, :, whole], result.at[part, :, whole], sems.at[4 * part + q]
            )
            store.start()
            stores.append(store)
    for store in stores:
        store.wait()


def shaped(*shape):
    return jax.ShapeDtypeStruct(shape, jnp.float32)


def call(kernel, outs, scratch=(), far_in=False, far_out=False):
    far, here = pl.BlockSpec(memory_space=pltpu.HBM), pl.BlockSpec(memory_space=pltpu.VMEM)
    out_specs = [far if far_out else here] * len(outs) if isinstance(outs, list) else (far if far_out else here)

    def run(*values):
        return pl.pallas_call(
            kernel,
            out_shape=outs,
            in_specs=[far if far_in else here] * len(values),
            out_specs=out_specs,
            scratch_shapes=list(scratch),
            compiler_params=pltpu.CompilerParams(vmem_limit_bytes=8 << 20),
            cost_estimate=pl.CostEstimate(flops=100000, bytes_accessed=1000000, transcendentals=0),
        )(*values)

    return run


def local(sound_field, index_start, index_end):
    span_shape = shaped(9 * SUB, LANE)
    cells = SUB * CELLS
    piece = cells // 4
    inputs = (sound_field, index_start, index_end)
    own, snap, source, curve, end = call(
        open_kernel,
        [
            span_shape,
            shaped(3, PARTS, SUB, LANE),
            shaped(2, cells, LANE),
            shaped(cells, LANE),
            shaped(*index_end.shape),
        ],
        [pltpu.VMEM(v.shape, jnp.float32) for v in inputs[:2]] + [pltpu.SemaphoreType.DMA((3,))],
        far_in=True,
    )(*(pltpu.with_memory_space_constraint(v, pltpu.HBM) for v in inputs))
    packs = call(stow_kernel, [shaped(4, piece, LANE)] * 4)(source, curve, end)

    def flip(value, axis, d):
        return lax.ppermute(value, axis, [(i, i ^ d) for i in range(lax.axis_size(axis))])

    def pair(axis, bit, a, b):
        return call(lambda *refs: pair_kernel(axis, bit, *refs), span_shape)(a, b)

    def quad(axis, a, others):
        return call(lambda *refs: quad_kernel(axis, *refs), span_shape)(a, *others)

    c1 = flip(own, "c", 1)
    total = pair("c", 0, own, c1)
    zs = [flip(total, "z", d) for d in (1, 2, 3)]
    total = quad("z", total, zs)
    z4 = lax.ppermute(total, "z", [(i, 7 - i) for i in range(8)])
    total = pair("z", 2, total, z4)
    ys = [flip(total, "y", d) for d in (1, 2, 3)]
    bounds = call(
        close_kernel, [shaped(4, SUB, LANE)] * 4, [pltpu.VMEM((4, 4, SUB, LANE), jnp.float32)]
    )(own, snap, c1, *zs, z4, *ys)
    packs = [packs[0]] + [flip(packs[d], "xr", d) for d in (1, 2, 3)]
    turns = []
    for d in TURNS:
        turns.append(call(turn_kernel, shaped(LANE, LANE))(packs[d]))
    bounds = [bounds[0]] + [flip(bounds[d], "xr", d) for d in (1, 2, 3)]
    tiles = sound_field.shape[2] // LANE
    curve, plan = call(
        lambda *refs: plan_kernel(tiles, *refs),
        [shaped(cells, LANE), shaped(LEVEL0 + 6 * PER_LEVEL, SUB, LANE)],
        [pltpu.VMEM((4, LANE, LANE), jnp.float32)],
    )(*turns, packs[3])
    result = shaped(2, CELLS // 4, 4 * sound_field.shape[2])
    return call(
        cross_kernel,
        result,
        [
            pltpu.VMEM((4, 2, piece, LANE), jnp.float32),
            pltpu.VMEM((4, 2, LANE, LANE), jnp.float32),
            pltpu.VMEM((2, cells, LANE), jnp.float32),
            pltpu.VMEM(result.shape, jnp.float32),
            pltpu.SemaphoreType.DMA((8,)),
        ],
        far_out=True,
    )(*bounds, *packs, curve, plan)


TURNS = (0, 1, 2)


def solution(mesh):
    split = Mesh(mesh.devices.reshape(4, 8, 2, mesh.shape["xr"]), DEPTH + ("xr",))
    in_specs = (P(None, DEPTH, "xr"), P(DEPTH, "xr"), P(DEPTH, "xr"))
    out_specs = P(None, DEPTH + ("xr",), None)

    return jax.shard_map(local, mesh=split, in_specs=in_specs, out_specs=out_specs, check_vma=False)
```

```python
import jax
import jax.numpy as jnp
from jax import lax
from jax.experimental import pallas as pl
from jax.experimental.pallas import tpu as pltpu
from jax.sharding import Mesh
from jax.sharding import PartitionSpec as P

DEPTH = ("y", "z", "c")

DEPTH_STIFFNESS = 1.6
CROSS_STIFFNESS = 1.2
NUMER = complex(2.857, 0.004)
DENOM = complex(2.857, -0.004)

MIX = (NUMER / DENOM) ** 2

SUB = 8
LANE = 128
CELLS = 64
PARTS = 12


def constants(stiffness):
    slope = -0.5 / stiffness
    base = 2.0 - (1.0 / DENOM).real / stiffness - slope
    swing = -(1.0 / DENOM).imag / stiffness
    push = ((DENOM - NUMER) / (NUMER * DENOM * stiffness)).imag
    return base, slope, swing, push


def mul(a, b):
    return a[0] * b[0] - a[1] * b[1], a[0] * b[1] + a[1] * b[0]


def add(a, b):
    return a[0] + b[0], a[1] + b[1]


def sub(a, b):
    return a[0] - b[0], a[1] - b[1]


def scaled(a, s):
    return a[0] * s, a[1] * s


def pick(flag, yes, no):
    return [(jnp.where(flag, p[0], q[0]), jnp.where(flag, p[1], q[1])) for p, q in zip(yes, no)]


def compose(early, late):
    a00, a10, a01, a11, r0, r1 = early
    b00, b10, b01, b11, s0, s1 = late
    return [
        add(mul(b00, a00), mul(b01, a10)),
        add(mul(b10, a00), mul(b11, a10)),
        add(mul(b00, a01), mul(b01, a11)),
        add(mul(b10, a01), mul(b11, a11)),
        add(r0, add(mul(a00, s0), mul(a10, s1))),
        add(r1, add(mul(a01, s0), mul(a11, s1))),
    ]


def normal(state):
    f0, f1, g = state
    size = jnp.maximum(
        jnp.maximum(jnp.abs(f0[0]), jnp.abs(f0[1])), jnp.maximum(jnp.abs(f1[0]), jnp.abs(f1[1]))
    )
    scale = 1.0 / size
    return [scaled(f0, scale), scaled(f1, scale), scaled(g, scale)]


def advance(state, span):
    f0, f1, g = state
    t00, t10, t01, t11, s0, s1 = span
    return [
        add(mul(t00, f0), mul(t01, f1)),
        add(mul(t10, f0), mul(t11, f1)),
        add(g, add(mul(f0, s0), mul(f1, s1))),
    ]


def retreat(state, span):
    p0, p1, h = state
    t00, t10, t01, t11, s0, s1 = span
    q0 = sub(mul(t11, p0), mul(t01, p1))
    q1 = sub(mul(t00, p1), mul(t10, p0))
    return [q0, q1, add(h, add(mul(q0, s0), mul(q1, s1)))]


def meet(left, right):
    f0, f1, g = left
    p0, p1, h = right
    det = sub(mul(f1, p0), mul(f0, p1))
    scale = -1.0 / (det[0] * det[0] + det[1] * det[1])
    inverse = (det[0] * scale, -det[1] * scale)
    v0 = mul(add(mul(f0, h), mul(p0, g)), inverse)
    v1 = mul(add(mul(g, p1), mul(f1, h)), inverse)
    return v0, v1


def ends(like):
    zero = jnp.zeros_like(like)
    one = zero + 1.0
    return [(zero, zero), (one, zero), (zero, zero)], [(one, zero), (zero, zero), (zero, zero)]


SPREAD = 7


def read(ref):
    values = [ref[SUB * i : SUB * (i + 1), :] for i in range(9)] + [ref[pl.ds(SPREAD, SUB, stride=SUB), :]]
    t00, t10, along, s0, s1 = zip(values[0::2], values[1::2])
    scale = 1.0 / (t00[0] * t00[0] + t00[1] * t00[1] + t10[0] * t10[0] + t10[1] * t10[1])
    p, q = mul(along, t00), mul(along, t10)
    t01 = (p[0] - t10[0] * scale, p[1] + t10[1] * scale)
    t11 = (q[0] + t00[0] * scale, q[1] - t00[1] * scale)
    return [t00, t10, t01, t11, s0, s1]


def write(ref, span):
    t00, t10, t01, t11, s0, s1 = span
    scale = 1.0 / (t00[0] * t00[0] + t00[1] * t00[1] + t10[0] * t10[0] + t10[1] * t10[1])
    along = add(mul((t00[0], -t00[1]), t01), mul((t10[0], -t10[1]), t11))
    values = [*t00, *t10, *scaled(along, scale), *s0, *s1]
    for i in range(9):
        ref[SUB * i : SUB * (i + 1), :] = values[i]
    ref[pl.ds(SPREAD, SPREAD, stride=SUB), :] = values[9][:SPREAD]


def rows(k):
    return pl.ds(SUB * k, SUB)


def step(c, swing, now, past, u=None):
    if u is not None:
        past = sub(past, u)
    return (c * now[0] - (swing * now[1] + past[0]), c * now[1] + (swing * now[0] - past[1]))


def start_pair():
    zero = jnp.zeros((SUB, LANE), jnp.float32)
    one = zero + 1.0
    return [[(one, zero), (zero, zero)], [(zero, zero), (one, zero)]]


def still():
    zero = jnp.zeros((SUB, LANE), jnp.float32)
    return [(zero, zero), (zero, zero)]


def through(matrix, v0, v1):
    t00, t10, t01, t11 = matrix
    return add(mul(t00, v0), mul(t01, v1)), add(mul(t10, v0), mul(t11, v1))


def product(late, early):
    first = through(late, early[0], early[1])
    second = through(late, early[2], early[3])
    return [first[0], first[1], second[0], second[1]]


def sums_of(matrix, p0, p1):
    t00, t10, t01, t11 = matrix
    return sub(mul(t00, p1), mul(t10, p0)), sub(mul(t01, p1), mul(t11, p0))


def read_all(ref, first, count):
    return [(ref[first + 2 * i], ref[first + 2 * i + 1]) for i in range(count)]


def write_all(ref, first, parts):
    for i, part in enumerate(parts):
        ref[first + 2 * i] = part[0]
        ref[first + 2 * i + 1] = part[1]


def open_kernel(field, start, end, own, snap, source, curve, end_in, field_in, start_in, sems):
    base, slope, swing, _ = constants(DEPTH_STIFFNESS)
    piece = CELLS // 4
    loads = []
    for i in range(4):
        some = pl.ds(piece * i, piece)
        loads.append(pltpu.make_async_copy(start.at[some], start_in.at[some], sems.at[2 * i]))
        loads.append(pltpu.make_async_copy(field.at[:, some], field_in.at[:, some], sems.at[2 * i + 1]))
    loads.append(pltpu.make_async_copy(end, end_in, sems.at[8]))
    for load in loads:
        load.start()
    tiles = field.shape[2] // LANE
    zero = jnp.zeros((CELLS, LANE), jnp.float32)
    for t in range(tiles, SUB):
        spread = pl.ds(t, CELLS, stride=SUB)
        source[0, spread, :] = zero
        source[1, spread, :] = zero
        curve[spread, :] = zero + (base + 0.9 * slope)
    waves = start_pair()
    march = still()
    for i in range(4):
        loads[2 * i].wait()
        loads[2 * i + 1].wait()
        some = slice(piece * i, piece * (i + 1))
        for t in range(tiles):
            spread, cols = pl.ds(SUB * piece * i + t, piece, stride=SUB), slice(t * LANE, (t + 1) * LANE)
            curve[spread, :] = base + slope * start_in[some, cols]
            source[0, spread, :] = field_in[0, some, cols]
            source[1, spread, :] = field_in[1, some, cols]
        for k in range(piece * i, piece * (i + 1)):
            u, c = (source[0, rows(k), :], source[1, rows(k), :]), curve[rows(k), :]
            march = [march[1], step(c, swing, march[1], march[0], u)]
            waves = [[w[1], step(c, swing, w[1], w[0])] for w in waves]
        if i < 3:
            write_all(snap.at[i], 0, waves[0] + waves[1] + march)
    matrix = waves[0] + waves[1]
    write(own, matrix + list(sums_of(matrix, *march)))
    loads[8].wait()


def stow_kernel(source, curve, end, *packs):
    xbase, xslope, _, _ = constants(CROSS_STIFFNESS)
    tiles = end.shape[1] // LANE
    x = lax.axis_index("xr")
    count = CELLS // 4
    for d, pack in enumerate(packs):
        here = pl.ds(pl.multiple_of((x ^ d) * SUB * count, SUB * count), SUB * count)
        re, im = source[0, here, :], source[1, here, :]
        pack[0] = MIX.real * re - MIX.imag * im
        pack[1] = MIX.real * im + MIX.imag * re
        pack[2] = curve[here, :]
        first = pl.multiple_of((x ^ d) * count, count)
        for t in range(tiles):
            cols = slice(t * LANE, (t + 1) * LANE)
            pack[3, pl.ds(t, count, stride=SUB), :] = xbase + xslope * end[pl.ds(first, count), cols]
        for t in range(tiles, SUB):
            pack[3, pl.ds(t, count, stride=SUB), :] = jnp.zeros((count, LANE), jnp.float32) + (
                xbase + 0.9 * xslope
            )


def turn_kernel(pack, turned):
    turned[...] = pack[3].T


def pair_kernel(axis, bit, own, other, total):
    upper = ((lax.axis_index(axis) >> bit) & 1) == 1
    a, b = read(own), read(other)
    write(total, compose(pick(upper, b, a), pick(upper, a, b)))


def quad_kernel(axis, own, other1, other2, other3, total):
    place = lax.axis_index(axis)
    odd = (place & 1) == 1
    high = (place & 2) == 2
    a, r1, r2, r3 = read(own), read(other1), read(other2), read(other3)
    mine = compose(pick(odd, r1, a), pick(odd, a, r1))
    theirs = compose(pick(odd, r3, r2), pick(odd, r2, r3))
    write(total, compose(pick(high, theirs, mine), pick(high, mine, theirs)))


def descend_pair(left, right, upper, other):
    return (
        pick(upper, normal(advance(left, other)), left),
        pick(upper, right, normal(retreat(right, other))),
    )


def descend_quad(left, right, place, r1, r2, r3):
    odd = (place & 1) == 1
    high = (place & 2) == 2
    first, second = pick(odd, r3, r2), pick(odd, r2, r3)
    left = pick(high, normal(advance(normal(advance(left, first)), second)), left)
    right = pick(high, right, normal(retreat(normal(retreat(right, second)), first)))
    return descend_pair(left, right, odd, r1)


def brace_kernel(own, c1, z1, z2, z3, z4, before, after):
    z, c = lax.axis_index("z"), lax.axis_index("c")
    block, partner = read(own), read(c1)
    second, odd, high, fold = c == 1, (z & 1) == 1, (z & 2) == 2, (z & 4) == 4
    near, far = read(z1), read(z4)
    r2, r3 = read(z2), read(z3)
    pair = compose(pick(odd, r3, r2), pick(odd, r2, r3))
    zero = jnp.zeros((SUB, LANE), jnp.float32)
    one = zero + 1.0
    unit = [(one, zero), (zero, zero), (zero, zero), (one, zero), (zero, zero), (zero, zero)]
    low, up = unit, block
    for flag, other in ((second, partner), (odd, near), (high, pair), (fold, far)):
        low = pick(flag, compose(other, low), low)
        up = pick(flag, up, compose(up, other))
    write_all(before, 0, low)
    write_all(after, 0, up)


def close_kernel(before, after, snap, y1, y2, y3, bound0, bound1, bound2, bound3, bounds):
    x, y = lax.axis_index("xr"), lax.axis_index("y")
    left, right = ends(snap[0, 0])
    left, right = descend_quad(left, right, y, read(y1), read(y2), read(y3))
    left = normal(advance(left, read_all(before, 0, 6)))
    right = normal(retreat(right, read_all(after, 0, 6)))
    v0, v1 = meet(left, right)
    used = lax.broadcasted_iota(jnp.int32, (SUB, LANE), 0) < SPREAD
    for i in range(4):
        a, b = v0, v1
        if i:
            span = read_all(snap.at[i - 1], 0, 6)
            a, b = through(span[:4], v0, v1)
            a, b = add(a, span[4]), add(b, span[5])
        for j, part in enumerate((a, b)):
            bounds[i, 2 * j] = jnp.where(used, MIX.real * part[0] - MIX.imag * part[1], 0.0)
            bounds[i, 2 * j + 1] = jnp.where(used, MIX.real * part[1] + MIX.imag * part[0], 0.0)
    for d, bound in enumerate((bound0, bound1, bound2, bound3)):
        bound[...] = bounds[x ^ d]


LEVELS = ((0, 1), (1, 1), (1, 2), (1, 4), (0, 2), (0, 4))
HALF = CELLS // 2
LATE, WHOLE, SOLVE, OWN, LEVEL0, PER_LEVEL = 8, 16, 24, 32, 36, 16


def upper_of(axis, stride):
    return (lax.broadcasted_iota(jnp.int32, (SUB, LANE), axis) & stride) == stride


def swapped(v, axis, stride, upper):
    size = SUB if axis == 0 else LANE
    down = pltpu.roll(v, stride, axis)
    if 2 * stride == size:
        return down
    return jnp.where(upper, down, pltpu.roll(v, size - stride, axis))


def swapped_all(parts, axis, stride, upper):
    return [(swapped(p[0], axis, stride, upper), swapped(p[1], axis, stride, upper)) for p in parts]


def middle(bound, pack, mid):
    _, _, swing, push = constants(DEPTH_STIFFNESS)
    past, now = (bound[0], bound[1]), (bound[2], bound[3])
    for k in range(CELLS // 4):
        u, c = (pack[0, rows(k), :], pack[1, rows(k), :]), pack[2, rows(k), :]
        mid[0, rows(k), :] = u[0] - push * now[1]
        mid[1, rows(k), :] = u[1] + push * now[0]
        past, now = now, step(c, swing, now, past, u)


def plan_kernel(*refs):
    tiles, bound, pack, (turn0, turn2, pack1, pack3) = refs[0], refs[1], refs[2], refs[3:7]
    curve, plan, first, whole, mid = refs[7:]
    middle(bound, pack, mid)
    first[0] = mid[0].T
    first[1] = mid[1].T
    _, _, swing, _ = constants(CROSS_STIFFNESS)
    x = lax.axis_index("xr")
    whole[x] = turn0[...]
    whole[x ^ 1] = pack1[3].T
    whole[x ^ 2] = turn2[...]
    whole[x ^ 3] = pack3[3].T
    for q in range(4):
        for h in range(2):
            curve[pl.ds(2 * q + h, CELLS, stride=SUB), :] = whole[q, CELLS * h : CELLS * (h + 1), :]
    halves = [start_pair(), start_pair()]
    for k in range(HALF):
        for h in range(2):
            c = curve[rows(k + HALF * h), :]
            halves[h] = [[w[1], step(c, swing, w[1], w[0])] for w in halves[h]]
    early, late = (w[0] + w[1] for w in halves)
    write_all(plan, 0, early)
    write_all(plan, LATE, late)
    matrix = product(late, early)
    write_all(plan, WHOLE, matrix)
    lane = lax.broadcasted_iota(jnp.int32, (SUB, LANE), 1)
    unit = start_pair()
    unit = unit[0] + unit[1]
    matrix = pick((lane & 7) >= tiles, unit, matrix)
    total = matrix
    stages = []
    for i, (axis, stride) in enumerate(LEVELS):
        upper = upper_of(axis, stride)
        other = swapped_all(total, axis, stride, upper)
        low = pick(upper, other, total)
        stages.append((upper, other))
        if i < 5:
            write_all(plan, LEVEL0 + PER_LEVEL * i, low)
            total = product(pick(upper, total, other), low)
    zero = jnp.zeros((SUB, LANE), jnp.float32)
    one = zero + 1.0
    left, right = [(zero, zero), (one, zero)], [(one, zero), (zero, zero)]
    left_weights, right_weights = [], []

    def rescale(pair, weights):
        size = jnp.maximum(
            jnp.maximum(jnp.abs(pair[0][0]), jnp.abs(pair[0][1])),
            jnp.maximum(jnp.abs(pair[1][0]), jnp.abs(pair[1][1])),
        )
        scale = 1.0 / size
        return [scaled(p, scale) for p in pair], [[scaled(w, scale) for w in ws] for ws in weights]

    for upper, other in reversed(stages):
        gone = list(through(other, left[0], left[1]))
        left_weights.append([scaled(p, jnp.where(upper, 1.0, 0.0)) for p in left])
        left, left_weights = rescale(pick(upper, gone, left), left_weights)
        t00, t10, t01, t11 = other
        back = [sub(mul(t11, right[0]), mul(t01, right[1])), sub(mul(t00, right[1]), mul(t10, right[0]))]
        right_weights.append([scaled(p, jnp.where(upper, 0.0, 1.0)) for p in back])
        right, right_weights = rescale(pick(upper, right, back), right_weights)
    t00, t10, t01, t11 = matrix
    right = [sub(mul(t11, right[0]), mul(t01, right[1])), sub(mul(t00, right[1]), mul(t10, right[0]))]
    right_weights.append(right)
    right, right_weights = rescale(right, right_weights)
    det = sub(mul(left[1], right[0]), mul(left[0], right[1]))
    scale = -1.0 / (det[0] * det[0] + det[1] * det[1])
    inverse = (det[0] * scale, -det[1] * scale)
    write_all(plan, SOLVE, [mul(p, inverse) for p in (left[0], right[0], right[1], left[1])])
    write_all(plan, OWN, right_weights[-1])
    for i in range(6):
        write_all(plan, LEVEL0 + PER_LEVEL * i + 8, left_weights[5 - i] + right_weights[5 - i])


def cross_kernel(*refs):
    bounds, packs, curve, plan, first, (result, mid, turned, source, out, sems) = (
        refs[:3], refs[3:6], refs[6], refs[7], refs[8], refs[9:],
    )
    tiles = result.shape[2] // LANE // 4
    x = lax.axis_index("xr")
    lines = CELLS // 4
    turned[x, 0] = first[0]
    turned[x, 1] = first[1]
    for d in range(1, 4):
        middle(bounds[d - 1], packs[d - 1], mid.at[d - 1])
        turned[x ^ d, 0] = mid[d - 1, 0].T
        turned[x ^ d, 1] = mid[d - 1, 1].T
    _, _, swing, push = constants(CROSS_STIFFNESS)
    for q in range(4):
        for h in range(2):
            spread = pl.ds(2 * q + h, CELLS, stride=SUB)
            half = slice(CELLS * h, CELLS * (h + 1))
            source[0, spread, :] = turned[q, 0, half, :]
            source[1, spread, :] = turned[q, 1, half, :]

    def cell(k):
        return (source[0, rows(k), :], source[1, rows(k), :]), curve[rows(k), :]

    marches = [still(), still()]
    for k in range(HALF):
        for h in range(2):
            u, c = cell(k + HALF * h)
            past, now = marches[h]
            marches[h] = [now, step(c, swing, now, past, u)]
    early, late, matrix = (read_all(plan, first, 4) for first in (0, LATE, WHOLE))
    end0, end1 = through(late, *marches[0])
    end0, end1 = add(end0, marches[1][0]), add(end1, marches[1][1])
    valid = (lax.broadcasted_iota(jnp.int32, (SUB, LANE), 1) & 7) < tiles
    zero = jnp.zeros((SUB, LANE), jnp.float32)
    sums = [(jnp.where(valid, s[0], zero), jnp.where(valid, s[1], zero)) for s in sums_of(matrix, end0, end1)]
    w0, w1 = read_all(plan, OWN, 2)
    g, h = (zero, zero), add(mul(w0, sums[0]), mul(w1, sums[1]))
    for i, (axis, stride) in enumerate(LEVELS):
        upper = upper_of(axis, stride)
        other = swapped_all(sums, axis, stride, upper)
        l0, l1, r0, r1 = read_all(plan, LEVEL0 + PER_LEVEL * i + 8, 4)
        g = add(g, add(mul(l0, other[0]), mul(l1, other[1])))
        h = add(h, add(mul(r0, other[0]), mul(r1, other[1])))
        if i < 5:
            t00, t10, t01, t11 = read_all(plan, LEVEL0 + PER_LEVEL * i, 4)
            low, high = pick(upper, other, sums), pick(upper, sums, other)
            sums = [
                add(low[0], add(mul(t00, high[0]), mul(t10, high[1]))),
                add(low[1], add(mul(t01, high[0]), mul(t11, high[1]))),
            ]
    f0, p0, p1, f1 = read_all(plan, SOLVE, 4)
    v0 = add(mul(f0, h), mul(p0, g))
    v1 = add(mul(p1, g), mul(f1, h))
    half = through(early, v0, v1)
    states = [[v0, v1], [add(half[0], marches[0][0]), add(half[1], marches[0][1])]]
    for k in range(HALF):
        for h in range(2):
            u, c = cell(k + HALF * h)
            past, now = states[h]
            source[0, rows(k + HALF * h), :] = u[0] - push * now[1]
            source[1, rows(k + HALF * h), :] = u[1] + push * now[0]
            states[h] = [now, step(c, swing, now, past, u)]
    stores = []
    for q in range(4):
        for part in range(2):
            halves = [source[part, pl.ds(2 * q + h, CELLS, stride=SUB), :] for h in range(2)]
            turned[q, part] = jnp.concatenate(halves, axis=0).T
            for t in range(tiles):
                cols = slice((q * tiles + t) * LANE, (q * tiles + t + 1) * LANE)
                out[part, :, cols] = turned[q, part, pl.ds(t, lines, stride=SUB), :]
        whole = pl.ds(q * tiles * LANE, tiles * LANE)
        store = pltpu.make_async_copy(out.at[:, :, whole], result.at[:, :, whole], sems.at[q])
        store.start()
        stores.append(store)
    for store in stores:
        store.wait()


def shaped(*shape):
    return jax.ShapeDtypeStruct(shape, jnp.float32)


def call(kernel, outs, scratch=(), far_in=False, far_out=False):
    far, here = pl.BlockSpec(memory_space=pltpu.HBM), pl.BlockSpec(memory_space=pltpu.VMEM)
    out_specs = [far if far_out else here] * len(outs) if isinstance(outs, list) else (far if far_out else here)

    def run(*values):
        return pl.pallas_call(
            kernel,
            out_shape=outs,
            in_specs=[far if far_in else here] * len(values),
            out_specs=out_specs,
            scratch_shapes=list(scratch),
            compiler_params=pltpu.CompilerParams(vmem_limit_bytes=8 << 20),
            cost_estimate=pl.CostEstimate(flops=100000, bytes_accessed=1000000, transcendentals=0),
        )(*values)

    return run


def local(sound_field, index_start, index_end):
    span_shape = shaped(9 * SUB, LANE)
    cells = SUB * CELLS
    piece = cells // 4
    inputs = (sound_field, index_start, index_end)
    own, snap, source, curve, end = call(
        open_kernel,
        [
            span_shape,
            shaped(3, PARTS, SUB, LANE),
            shaped(2, cells, LANE),
            shaped(cells, LANE),
            shaped(*index_end.shape),
        ],
        [pltpu.VMEM(v.shape, jnp.float32) for v in inputs[:2]] + [pltpu.SemaphoreType.DMA((9,))],
        far_in=True,
    )(*(pltpu.with_memory_space_constraint(v, pltpu.HBM) for v in inputs))
    packs = call(stow_kernel, [shaped(4, piece, LANE)] * 4)(source, curve, end)

    def flip(value, axis, d):
        return lax.ppermute(value, axis, [(i, i ^ d) for i in range(lax.axis_size(axis))])

    def pair(axis, bit, a, b):
        return call(lambda *refs: pair_kernel(axis, bit, *refs), span_shape)(a, b)

    def quad(axis, a, others):
        return call(lambda *refs: quad_kernel(axis, *refs), span_shape)(a, *others)

    c1 = flip(own, "c", 1)
    total = pair("c", 0, own, c1)
    zs = [flip(total, "z", d) for d in (1, 2, 3)]
    total = quad("z", total, zs)
    z4 = lax.ppermute(total, "z", [(i, 7 - i) for i in range(8)])
    total = pair("z", 2, total, z4)
    ys = [flip(total, "y", d) for d in (1, 2, 3)]
    before, after = call(brace_kernel, [shaped(PARTS, SUB, LANE)] * 2)(own, c1, *zs, z4)
    bounds = call(
        close_kernel, [shaped(4, SUB, LANE)] * 4, [pltpu.VMEM((4, 4, SUB, LANE), jnp.float32)]
    )(before, after, snap, *ys)
    packs = [packs[0]] + [flip(packs[d], "xr", d) for d in (1, 2, 3)]
    turns = []
    for d in TURNS:
        turns.append(call(turn_kernel, shaped(LANE, LANE))(packs[d]))
    bounds = [bounds[0]] + [flip(bounds[d], "xr", d) for d in (1, 2, 3)]
    tiles = sound_field.shape[2] // LANE
    curve, plan, first = call(
        lambda *refs: plan_kernel(tiles, *refs),
        [shaped(cells, LANE), shaped(LEVEL0 + 6 * PER_LEVEL, SUB, LANE), shaped(2, LANE, LANE)],
        [pltpu.VMEM((4, LANE, LANE), jnp.float32), pltpu.VMEM((2, piece, LANE), jnp.float32)],
    )(bounds[0], packs[0], *turns, packs[1], packs[3])
    result = shaped(2, CELLS // 4, 4 * sound_field.shape[2])
    return call(
        cross_kernel,
        result,
        [
            pltpu.VMEM((3, 2, piece, LANE), jnp.float32),
            pltpu.VMEM((4, 2, LANE, LANE), jnp.float32),
            pltpu.VMEM((2, cells, LANE), jnp.float32),
            pltpu.VMEM(result.shape, jnp.float32),
            pltpu.SemaphoreType.DMA((4,)),
        ],
        far_out=True,
    )(*bounds[1:], *packs[1:], curve, plan, first)


TURNS = (0, 2)


def solution(mesh):
    split = Mesh(mesh.devices.reshape(4, 8, 2, mesh.shape["xr"]), DEPTH + ("xr",))
    in_specs = (P(None, DEPTH, "xr"), P(DEPTH, "xr"), P(DEPTH, "xr"))
    out_specs = P(None, DEPTH + ("xr",), None)

    return jax.shard_map(local, mesh=split, in_specs=in_specs, out_specs=out_specs, check_vma=False)
```

```python
import jax
import jax.numpy as jnp
from jax import lax
from jax.experimental import pallas as pl
from jax.experimental.pallas import tpu as pltpu
from jax.sharding import Mesh
from jax.sharding import PartitionSpec as P

DEPTH = ("y", "z", "c")

DEPTH_STIFFNESS = 1.6
CROSS_STIFFNESS = 1.2
NUMER = complex(2.857, 0.004)
DENOM = complex(2.857, -0.004)

MIX = (NUMER / DENOM) ** 2

SUB = 8
LANE = 128
CELLS = 64
PARTS = 12


def constants(stiffness):
    slope = -0.5 / stiffness
    base = 2.0 - (1.0 / DENOM).real / stiffness - slope
    swing = -(1.0 / DENOM).imag / stiffness
    push = ((DENOM - NUMER) / (NUMER * DENOM * stiffness)).imag
    return base, slope, swing, push


def mul(a, b):
    return a[0] * b[0] - a[1] * b[1], a[0] * b[1] + a[1] * b[0]


def add(a, b):
    return a[0] + b[0], a[1] + b[1]


def sub(a, b):
    return a[0] - b[0], a[1] - b[1]


def scaled(a, s):
    return a[0] * s, a[1] * s


def pick(flag, yes, no):
    return [(jnp.where(flag, p[0], q[0]), jnp.where(flag, p[1], q[1])) for p, q in zip(yes, no)]


def compose(early, late):
    a00, a10, a01, a11, r0, r1 = early
    b00, b10, b01, b11, s0, s1 = late
    return [
        add(mul(b00, a00), mul(b01, a10)),
        add(mul(b10, a00), mul(b11, a10)),
        add(mul(b00, a01), mul(b01, a11)),
        add(mul(b10, a01), mul(b11, a11)),
        add(r0, add(mul(a00, s0), mul(a10, s1))),
        add(r1, add(mul(a01, s0), mul(a11, s1))),
    ]


def normal(state):
    f0, f1, g = state
    size = jnp.maximum(
        jnp.maximum(jnp.abs(f0[0]), jnp.abs(f0[1])), jnp.maximum(jnp.abs(f1[0]), jnp.abs(f1[1]))
    )
    scale = 1.0 / size
    return [scaled(f0, scale), scaled(f1, scale), scaled(g, scale)]


def advance(state, span):
    f0, f1, g = state
    t00, t10, t01, t11, s0, s1 = span
    return [
        add(mul(t00, f0), mul(t01, f1)),
        add(mul(t10, f0), mul(t11, f1)),
        add(g, add(mul(f0, s0), mul(f1, s1))),
    ]


def retreat(state, span):
    p0, p1, h = state
    t00, t10, t01, t11, s0, s1 = span
    q0 = sub(mul(t11, p0), mul(t01, p1))
    q1 = sub(mul(t00, p1), mul(t10, p0))
    return [q0, q1, add(h, add(mul(q0, s0), mul(q1, s1)))]


def meet(left, right):
    f0, f1, g = left
    p0, p1, h = right
    det = sub(mul(f1, p0), mul(f0, p1))
    scale = -1.0 / (det[0] * det[0] + det[1] * det[1])
    inverse = (det[0] * scale, -det[1] * scale)
    v0 = mul(add(mul(f0, h), mul(p0, g)), inverse)
    v1 = mul(add(mul(g, p1), mul(f1, h)), inverse)
    return v0, v1


def ends(like):
    zero = jnp.zeros_like(like)
    one = zero + 1.0
    return [(zero, zero), (one, zero), (zero, zero)], [(one, zero), (zero, zero), (zero, zero)]


SPREAD = 7


def read(ref):
    values = [ref[SUB * i : SUB * (i + 1), :] for i in range(9)] + [ref[pl.ds(SPREAD, SUB, stride=SUB), :]]
    t00, t10, along, s0, s1 = zip(values[0::2], values[1::2])
    scale = 1.0 / (t00[0] * t00[0] + t00[1] * t00[1] + t10[0] * t10[0] + t10[1] * t10[1])
    p, q = mul(along, t00), mul(along, t10)
    t01 = (p[0] - t10[0] * scale, p[1] + t10[1] * scale)
    t11 = (q[0] + t00[0] * scale, q[1] - t00[1] * scale)
    return [t00, t10, t01, t11, s0, s1]


def write(ref, span):
    t00, t10, t01, t11, s0, s1 = span
    scale = 1.0 / (t00[0] * t00[0] + t00[1] * t00[1] + t10[0] * t10[0] + t10[1] * t10[1])
    along = add(mul((t00[0], -t00[1]), t01), mul((t10[0], -t10[1]), t11))
    values = [*t00, *t10, *scaled(along, scale), *s0, *s1]
    for i in range(9):
        ref[SUB * i : SUB * (i + 1), :] = values[i]
    ref[pl.ds(SPREAD, SPREAD, stride=SUB), :] = values[9][:SPREAD]


def rows(k):
    return pl.ds(SUB * k, SUB)


def step(c, swing, now, past, u=None):
    if u is not None:
        past = sub(past, u)
    return (c * now[0] - (swing * now[1] + past[0]), c * now[1] + (swing * now[0] - past[1]))


def start_pair():
    zero = jnp.zeros((SUB, LANE), jnp.float32)
    one = zero + 1.0
    return [[(one, zero), (zero, zero)], [(zero, zero), (one, zero)]]


def still():
    zero = jnp.zeros((SUB, LANE), jnp.float32)
    return [(zero, zero), (zero, zero)]


def through(matrix, v0, v1):
    t00, t10, t01, t11 = matrix
    return add(mul(t00, v0), mul(t01, v1)), add(mul(t10, v0), mul(t11, v1))


def product(late, early):
    first = through(late, early[0], early[1])
    second = through(late, early[2], early[3])
    return [first[0], first[1], second[0], second[1]]


def sums_of(matrix, p0, p1):
    t00, t10, t01, t11 = matrix
    return sub(mul(t00, p1), mul(t10, p0)), sub(mul(t01, p1), mul(t11, p0))


def read_all(ref, first, count):
    return [(ref[first + 2 * i], ref[first + 2 * i + 1]) for i in range(count)]


def write_all(ref, first, parts):
    for i, part in enumerate(parts):
        ref[first + 2 * i] = part[0]
        ref[first + 2 * i + 1] = part[1]


def open_kernel(field, start, end, own, snap, source, curve, end_in, field_in, start_in, sems):
    base, slope, swing, _ = constants(DEPTH_STIFFNESS)
    piece = CELLS // 4
    loads = []
    for i in range(4):
        some = pl.ds(piece * i, piece)
        loads.append(pltpu.make_async_copy(start.at[some], start_in.at[some], sems.at[2 * i]))
        loads.append(pltpu.make_async_copy(field.at[:, some], field_in.at[:, some], sems.at[2 * i + 1]))
    loads.append(pltpu.make_async_copy(end, end_in, sems.at[8]))
    for load in loads:
        load.start()
    tiles = field.shape[2] // LANE
    zero = jnp.zeros((CELLS, LANE), jnp.float32)
    for t in range(tiles, SUB):
        spread = pl.ds(t, CELLS, stride=SUB)
        source[0, spread, :] = zero
        source[1, spread, :] = zero
        curve[spread, :] = zero + (base + 0.9 * slope)
    waves = start_pair()
    march = still()
    for i in range(4):
        loads[2 * i].wait()
        loads[2 * i + 1].wait()
        some = slice(piece * i, piece * (i + 1))
        for t in range(tiles):
            spread, cols = pl.ds(SUB * piece * i + t, piece, stride=SUB), slice(t * LANE, (t + 1) * LANE)
            curve[spread, :] = base + slope * start_in[some, cols]
            source[0, spread, :] = field_in[0, some, cols]
            source[1, spread, :] = field_in[1, some, cols]
        for k in range(piece * i, piece * (i + 1)):
            u, c = (source[0, rows(k), :], source[1, rows(k), :]), curve[rows(k), :]
            march = [march[1], step(c, swing, march[1], march[0], u)]
            waves = [[w[1], step(c, swing, w[1], w[0])] for w in waves]
        if i < 3:
            write_all(snap.at[i], 0, waves[0] + waves[1] + march)
    matrix = waves[0] + waves[1]
    write(own, matrix + list(sums_of(matrix, *march)))
    loads[8].wait()


def stow_kernel(source, curve, end, *packs):
    xbase, xslope, _, _ = constants(CROSS_STIFFNESS)
    tiles = end.shape[1] // LANE
    x = lax.axis_index("xr")
    count = CELLS // 4
    for d, pack in enumerate(packs):
        here = pl.ds(pl.multiple_of((x ^ d) * SUB * count, SUB * count), SUB * count)
        re, im = source[0, here, :], source[1, here, :]
        pack[0] = MIX.real * re - MIX.imag * im
        pack[1] = MIX.real * im + MIX.imag * re
        pack[2] = curve[here, :]
        first = pl.multiple_of((x ^ d) * count, count)
        for t in range(tiles):
            cols = slice(t * LANE, (t + 1) * LANE)
            pack[3, pl.ds(t, count, stride=SUB), :] = xbase + xslope * end[pl.ds(first, count), cols]
        for t in range(tiles, SUB):
            pack[3, pl.ds(t, count, stride=SUB), :] = jnp.zeros((count, LANE), jnp.float32) + (
                xbase + 0.9 * xslope
            )


def turn_kernel(pack, turned):
    turned[...] = pack[3].T


def pair_kernel(axis, bit, own, other, total):
    upper = ((lax.axis_index(axis) >> bit) & 1) == 1
    a, b = read(own), read(other)
    write(total, compose(pick(upper, b, a), pick(upper, a, b)))


def quad_kernel(axis, own, other1, other2, other3, total):
    place = lax.axis_index(axis)
    odd = (place & 1) == 1
    high = (place & 2) == 2
    a, r1, r2, r3 = read(own), read(other1), read(other2), read(other3)
    mine = compose(pick(odd, r1, a), pick(odd, a, r1))
    theirs = compose(pick(odd, r3, r2), pick(odd, r2, r3))
    write(total, compose(pick(high, theirs, mine), pick(high, mine, theirs)))


def descend_pair(left, right, upper, other):
    return (
        pick(upper, normal(advance(left, other)), left),
        pick(upper, right, normal(retreat(right, other))),
    )


def descend_quad(left, right, place, r1, r2, r3):
    odd = (place & 1) == 1
    high = (place & 2) == 2
    first, second = pick(odd, r3, r2), pick(odd, r2, r3)
    left = pick(high, normal(advance(normal(advance(left, first)), second)), left)
    right = pick(high, right, normal(retreat(normal(retreat(right, second)), first)))
    return descend_pair(left, right, odd, r1)


def brace_kernel(own, c1, z1, z2, z3, z4, before, after):
    z, c = lax.axis_index("z"), lax.axis_index("c")
    block, partner = read(own), read(c1)
    second, odd, high, fold = c == 1, (z & 1) == 1, (z & 2) == 2, (z & 4) == 4
    near, far = read(z1), read(z4)
    r2, r3 = read(z2), read(z3)
    pair = compose(pick(odd, r3, r2), pick(odd, r2, r3))
    zero = jnp.zeros((SUB, LANE), jnp.float32)
    one = zero + 1.0
    unit = [(one, zero), (zero, zero), (zero, zero), (one, zero), (zero, zero), (zero, zero)]
    low, up = unit, block
    for flag, other in ((second, partner), (odd, near), (high, pair), (fold, far)):
        low = pick(flag, compose(other, low), low)
        up = pick(flag, up, compose(up, other))
    write_all(before, 0, low)
    write_all(after, 0, up)


def close_kernel(before, after, snap, y1, y2, y3, bound0, bound1, bound2, bound3, bounds):
    x, y = lax.axis_index("xr"), lax.axis_index("y")
    left, right = ends(snap[0, 0])
    left, right = descend_quad(left, right, y, read(y1), read(y2), read(y3))
    left = normal(advance(left, read_all(before, 0, 6)))
    right = normal(retreat(right, read_all(after, 0, 6)))
    v0, v1 = meet(left, right)
    used = lax.broadcasted_iota(jnp.int32, (SUB, LANE), 0) < SPREAD
    for i in range(4):
        a, b = v0, v1
        if i:
            span = read_all(snap.at[i - 1], 0, 6)
            a, b = through(span[:4], v0, v1)
            a, b = add(a, span[4]), add(b, span[5])
        for j, part in enumerate((a, b)):
            bounds[i, 2 * j] = jnp.where(used, MIX.real * part[0] - MIX.imag * part[1], 0.0)
            bounds[i, 2 * j + 1] = jnp.where(used, MIX.real * part[1] + MIX.imag * part[0], 0.0)
    for d, bound in enumerate((bound0, bound1, bound2, bound3)):
        bound[...] = bounds[x ^ d]


LEVELS = ((0, 1), (1, 1), (1, 2), (1, 4), (0, 2), (0, 4))
HALF = CELLS // 2
LATE, WHOLE, SOLVE, OWN, LEVEL0, PER_LEVEL = 8, 16, 24, 32, 36, 16


def upper_of(axis, stride):
    return (lax.broadcasted_iota(jnp.int32, (SUB, LANE), axis) & stride) == stride


def swapped(v, axis, stride, upper):
    size = SUB if axis == 0 else LANE
    down = pltpu.roll(v, stride, axis)
    if 2 * stride == size:
        return down
    return jnp.where(upper, down, pltpu.roll(v, size - stride, axis))


def swapped_all(parts, axis, stride, upper):
    return [(swapped(p[0], axis, stride, upper), swapped(p[1], axis, stride, upper)) for p in parts]


def middle(bound, pack, mid):
    _, _, swing, push = constants(DEPTH_STIFFNESS)
    past, now = (bound[0], bound[1]), (bound[2], bound[3])
    for k in range(CELLS // 4):
        u, c = (pack[0, rows(k), :], pack[1, rows(k), :]), pack[2, rows(k), :]
        mid[0, rows(k), :] = u[0] - push * now[1]
        mid[1, rows(k), :] = u[1] + push * now[0]
        past, now = now, step(c, swing, now, past, u)


def plan_kernel(*refs):
    tiles, bound, pack, turns, last = refs[0], refs[1], refs[2], refs[3:6], refs[6]
    curve, plan, first, whole, mid = refs[7:]
    middle(bound, pack, mid)
    first[0] = mid[0].T
    first[1] = mid[1].T
    _, _, swing, _ = constants(CROSS_STIFFNESS)
    x = lax.axis_index("xr")
    for d in range(4):
        whole[x ^ d] = turns[d][...] if d < 3 else last[3].T
    for q in range(4):
        for h in range(2):
            curve[pl.ds(2 * q + h, CELLS, stride=SUB), :] = whole[q, CELLS * h : CELLS * (h + 1), :]
    halves = [start_pair(), start_pair()]
    for k in range(HALF):
        for h in range(2):
            c = curve[rows(k + HALF * h), :]
            halves[h] = [[w[1], step(c, swing, w[1], w[0])] for w in halves[h]]
    early, late = (w[0] + w[1] for w in halves)
    write_all(plan, 0, early)
    write_all(plan, LATE, late)
    matrix = product(late, early)
    write_all(plan, WHOLE, matrix)
    lane = lax.broadcasted_iota(jnp.int32, (SUB, LANE), 1)
    unit = start_pair()
    unit = unit[0] + unit[1]
    matrix = pick((lane & 7) >= tiles, unit, matrix)
    total = matrix
    stages = []
    for i, (axis, stride) in enumerate(LEVELS):
        upper = upper_of(axis, stride)
        other = swapped_all(total, axis, stride, upper)
        low = pick(upper, other, total)
        stages.append((upper, other))
        if i < 5:
            write_all(plan, LEVEL0 + PER_LEVEL * i, low)
            total = product(pick(upper, total, other), low)
    zero = jnp.zeros((SUB, LANE), jnp.float32)
    one = zero + 1.0
    left, right = [(zero, zero), (one, zero)], [(one, zero), (zero, zero)]
    left_weights, right_weights = [], []

    def rescale(pair, weights):
        size = jnp.maximum(
            jnp.maximum(jnp.abs(pair[0][0]), jnp.abs(pair[0][1])),
            jnp.maximum(jnp.abs(pair[1][0]), jnp.abs(pair[1][1])),
        )
        scale = 1.0 / size
        return [scaled(p, scale) for p in pair], [[scaled(w, scale) for w in ws] for ws in weights]

    for upper, other in reversed(stages):
        gone = list(through(other, left[0], left[1]))
        left_weights.append([scaled(p, jnp.where(upper, 1.0, 0.0)) for p in left])
        left, left_weights = rescale(pick(upper, gone, left), left_weights)
        t00, t10, t01, t11 = other
        back = [sub(mul(t11, right[0]), mul(t01, right[1])), sub(mul(t00, right[1]), mul(t10, right[0]))]
        right_weights.append([scaled(p, jnp.where(upper, 0.0, 1.0)) for p in back])
        right, right_weights = rescale(pick(upper, right, back), right_weights)
    t00, t10, t01, t11 = matrix
    right = [sub(mul(t11, right[0]), mul(t01, right[1])), sub(mul(t00, right[1]), mul(t10, right[0]))]
    right_weights.append(right)
    right, right_weights = rescale(right, right_weights)
    det = sub(mul(left[1], right[0]), mul(left[0], right[1]))
    scale = -1.0 / (det[0] * det[0] + det[1] * det[1])
    inverse = (det[0] * scale, -det[1] * scale)
    write_all(plan, SOLVE, [mul(p, inverse) for p in (left[0], right[0], right[1], left[1])])
    write_all(plan, OWN, right_weights[-1])
    for i in range(6):
        write_all(plan, LEVEL0 + PER_LEVEL * i + 8, left_weights[5 - i] + right_weights[5 - i])


def cross_kernel(*refs):
    bounds, packs, curve, plan, first, (result, mid, turned, source, out, sems) = (
        refs[:3], refs[3:6], refs[6], refs[7], refs[8], refs[9:],
    )
    tiles = result.shape[2] // LANE // 4
    x = lax.axis_index("xr")
    lines = CELLS // 4
    turned[x, 0] = first[0]
    turned[x, 1] = first[1]
    for d in range(1, 4):
        middle(bounds[d - 1], packs[d - 1], mid.at[d - 1])
        turned[x ^ d, 0] = mid[d - 1, 0].T
        turned[x ^ d, 1] = mid[d - 1, 1].T
    _, _, swing, push = constants(CROSS_STIFFNESS)
    for q in range(4):
        for h in range(2):
            spread = pl.ds(2 * q + h, CELLS, stride=SUB)
            half = slice(CELLS * h, CELLS * (h + 1))
            source[0, spread, :] = turned[q, 0, half, :]
            source[1, spread, :] = turned[q, 1, half, :]

    def cell(k):
        return (source[0, rows(k), :], source[1, rows(k), :]), curve[rows(k), :]

    marches = [still(), still()]
    for k in range(HALF):
        for h in range(2):
            u, c = cell(k + HALF * h)
            past, now = marches[h]
            marches[h] = [now, step(c, swing, now, past, u)]
    early, late, matrix = (read_all(plan, first, 4) for first in (0, LATE, WHOLE))
    end0, end1 = through(late, *marches[0])
    end0, end1 = add(end0, marches[1][0]), add(end1, marches[1][1])
    valid = (lax.broadcasted_iota(jnp.int32, (SUB, LANE), 1) & 7) < tiles
    zero = jnp.zeros((SUB, LANE), jnp.float32)
    sums = [(jnp.where(valid, s[0], zero), jnp.where(valid, s[1], zero)) for s in sums_of(matrix, end0, end1)]
    w0, w1 = read_all(plan, OWN, 2)
    g, h = (zero, zero), add(mul(w0, sums[0]), mul(w1, sums[1]))
    for i, (axis, stride) in enumerate(LEVELS):
        upper = upper_of(axis, stride)
        other = swapped_all(sums, axis, stride, upper)
        l0, l1, r0, r1 = read_all(plan, LEVEL0 + PER_LEVEL * i + 8, 4)
        g = add(g, add(mul(l0, other[0]), mul(l1, other[1])))
        h = add(h, add(mul(r0, other[0]), mul(r1, other[1])))
        if i < 5:
            t00, t10, t01, t11 = read_all(plan, LEVEL0 + PER_LEVEL * i, 4)
            low, high = pick(upper, other, sums), pick(upper, sums, other)
            sums = [
                add(low[0], add(mul(t00, high[0]), mul(t10, high[1]))),
                add(low[1], add(mul(t01, high[0]), mul(t11, high[1]))),
            ]
    f0, p0, p1, f1 = read_all(plan, SOLVE, 4)
    v0 = add(mul(f0, h), mul(p0, g))
    v1 = add(mul(p1, g), mul(f1, h))
    half = through(early, v0, v1)
    states = [[v0, v1], [add(half[0], marches[0][0]), add(half[1], marches[0][1])]]
    for k in range(HALF):
        for h in range(2):
            u, c = cell(k + HALF * h)
            past, now = states[h]
            source[0, rows(k + HALF * h), :] = u[0] - push * now[1]
            source[1, rows(k + HALF * h), :] = u[1] + push * now[0]
            states[h] = [now, step(c, swing, now, past, u)]
    stores = []
    for q in range(4):
        for part in range(2):
            halves = [source[part, pl.ds(2 * q + h, CELLS, stride=SUB), :] for h in range(2)]
            turned[q, part] = jnp.concatenate(halves, axis=0).T
            for t in range(tiles):
                cols = slice((q * tiles + t) * LANE, (q * tiles + t + 1) * LANE)
                out[part, :, cols] = turned[q, part, pl.ds(t, lines, stride=SUB), :]
            whole = pl.ds(q * tiles * LANE, tiles * LANE)
            store = pltpu.make_async_copy(
                out.at[part, :, whole], result.at[part, :, whole], sems.at[4 * part + q]
            )
            store.start()
            stores.append(store)
    for store in stores:
        store.wait()


def shaped(*shape):
    return jax.ShapeDtypeStruct(shape, jnp.float32)


def call(kernel, outs, scratch=(), far_in=False, far_out=False):
    far, here = pl.BlockSpec(memory_space=pltpu.HBM), pl.BlockSpec(memory_space=pltpu.VMEM)
    out_specs = [far if far_out else here] * len(outs) if isinstance(outs, list) else (far if far_out else here)

    def run(*values):
        return pl.pallas_call(
            kernel,
            out_shape=outs,
            in_specs=[far if far_in else here] * len(values),
            out_specs=out_specs,
            scratch_shapes=list(scratch),
            compiler_params=pltpu.CompilerParams(vmem_limit_bytes=8 << 20),
            cost_estimate=pl.CostEstimate(flops=100000, bytes_accessed=1000000, transcendentals=0),
        )(*values)

    return run


def local(sound_field, index_start, index_end):
    span_shape = shaped(9 * SUB, LANE)
    cells = SUB * CELLS
    piece = cells // 4
    inputs = (sound_field, index_start, index_end)
    own, snap, source, curve, end = call(
        open_kernel,
        [
            span_shape,
            shaped(3, PARTS, SUB, LANE),
            shaped(2, cells, LANE),
            shaped(cells, LANE),
            shaped(*index_end.shape),
        ],
        [pltpu.VMEM(v.shape, jnp.float32) for v in inputs[:2]] + [pltpu.SemaphoreType.DMA((9,))],
        far_in=True,
    )(*(pltpu.with_memory_space_constraint(v, pltpu.HBM) for v in inputs))
    packs = call(stow_kernel, [shaped(4, piece, LANE)] * 4)(source, curve, end)

    def flip(value, axis, d):
        return lax.ppermute(value, axis, [(i, i ^ d) for i in range(lax.axis_size(axis))])

    def pair(axis, bit, a, b):
        return call(lambda *refs: pair_kernel(axis, bit, *refs), span_shape)(a, b)

    def quad(axis, a, others):
        return call(lambda *refs: quad_kernel(axis, *refs), span_shape)(a, *others)

    c1 = flip(own, "c", 1)
    total = pair("c", 0, own, c1)
    zs = [flip(total, "z", d) for d in (1, 2, 3)]
    total = quad("z", total, zs)
    z4 = lax.ppermute(total, "z", [(i, 7 - i) for i in range(8)])
    total = pair("z", 2, total, z4)
    ys = [flip(total, "y", d) for d in (1, 2, 3)]
    before, after = call(brace_kernel, [shaped(PARTS, SUB, LANE)] * 2)(own, c1, *zs, z4)
    bounds = call(
        close_kernel, [shaped(4, SUB, LANE)] * 4, [pltpu.VMEM((4, 4, SUB, LANE), jnp.float32)]
    )(before, after, snap, *ys)
    packs = [packs[0]] + [flip(packs[d], "xr", d) for d in (1, 2, 3)]
    turns = []
    for d in TURNS:
        turns.append(call(turn_kernel, shaped(LANE, LANE))(packs[d]))
    bounds = [bounds[0]] + [flip(bounds[d], "xr", d) for d in (1, 2, 3)]
    tiles = sound_field.shape[2] // LANE
    curve, plan, first = call(
        lambda *refs: plan_kernel(tiles, *refs),
        [shaped(cells, LANE), shaped(LEVEL0 + 6 * PER_LEVEL, SUB, LANE), shaped(2, LANE, LANE)],
        [pltpu.VMEM((4, LANE, LANE), jnp.float32), pltpu.VMEM((2, piece, LANE), jnp.float32)],
    )(bounds[0], packs[0], *turns, packs[3])
    result = shaped(2, CELLS // 4, 4 * sound_field.shape[2])
    return call(
        cross_kernel,
        result,
        [
            pltpu.VMEM((3, 2, piece, LANE), jnp.float32),
            pltpu.VMEM((4, 2, LANE, LANE), jnp.float32),
            pltpu.VMEM((2, cells, LANE), jnp.float32),
            pltpu.VMEM(result.shape, jnp.float32),
            pltpu.SemaphoreType.DMA((8,)),
        ],
        far_out=True,
    )(*bounds[1:], *packs[1:], curve, plan, first)


TURNS = (0, 1, 2)


def solution(mesh):
    split = Mesh(mesh.devices.reshape(4, 8, 2, mesh.shape["xr"]), DEPTH + ("xr",))
    in_specs = (P(None, DEPTH, "xr"), P(DEPTH, "xr"), P(DEPTH, "xr"))
    out_specs = P(None, DEPTH + ("xr",), None)

    return jax.shard_map(local, mesh=split, in_specs=in_specs, out_specs=out_specs, check_vma=False)
```
